32 devices in a mesh: ens: 2 (over y), node: 4 (over z), feat: 4 (over x, core).
Axes of the slice: x: 2, y: 2, z: 4, core: 2. Of those that a mesh axis runs over, the one named last changes fastest.
Arguments:
- nodes: bfloat16 [4096, 512], P(('ens', 'node', 'feat')), parts along dimension 0, may hold values from -6 to 6
- edges: bfloat16 [65536, 512], P(('ens', 'node', 'feat')), parts along dimension 0, may hold values from -6 to 6
- near_table: int32 [32, 5, 48], P(('ens', 'node', 'feat')), parts along dimension 0, may hold values from 0 to 127, as said below
- far_table: int32 [32, 16, 2], P(('ens', 'node', 'feat')), parts along dimension 0, may hold values from 0 to 127, as said below
- edge_sender: int32 [65536], P(('ens', 'node', 'feat')), parts along dimension 0, may hold values from 0 to 271, as said below
- edge_receiver: int32 [65536], P(('ens', 'node', 'feat')), parts along dimension 0, may hold values from 0 to 271, as said below
- edge_w1: bfloat16 [2, 1536, 512], replicated, may hold values from -0.15625 to 0.15625
- edge_b1: float32 [2, 512], replicated, may hold values from -4 to 4
- edge_w2: bfloat16 [2, 512, 512], replicated, may hold values from -0.25 to 0.25
- edge_gain: float32 [2, 512], replicated, may hold values from 0.5 to 1.5
- edge_shift: float32 [2, 512], replicated, may hold values from -3 to 3
- node_w1: bfloat16 [2, 1024, 512], replicated, may hold values from -0.1875 to 0.1875
- node_b1: float32 [2, 512], replicated, may hold values from -4 to 4
- node_w2: bfloat16 [2, 512, 512], replicated, may hold values from -0.25 to 0.25
- node_gain: float32 [2, 512], replicated, may hold values from 0.5 to 1.5
- node_shift: float32 [2, 512], replicated, may hold values from -3 to 3
Outputs:
- node_out: bfloat16 [4096, 512], P(('ens', 'node', 'feat')), parts along dimension 0
- edge_out: bfloat16 [65536, 512], P(('ens', 'node', 'feat')), parts along dimension 0
The draws below stay inside these ranges and needn't reach their ends.
There are 2 independent parts, one for each index of `ens`. The reference program is written for one: setup_inputs(seed, part) draws one part's arguments, and reference() takes and returns one part's arrays. A program takes and returns all parts, laid end to end along the dimension named above; an argument that names none is the same for every part. Nothing has to cross between parts.
Inputs may be any that keep to these rules, and one draw needn't show every extreme that they name: `near_table`: entry [p, k, c] is a row among the 128 nodes of device p. `far_table`: entry [p, q, c] is a row among the 128 nodes of device p. `edge_sender`: an edge's entry names a near slot (below (5) * 48) or a far slot of the tables as the steps read them. `edge_receiver`: an edge's entry names a near slot (below (5) * 48) or a far slot of the tables as the steps read them.
All inputs are finite; a program needn't handle non-finite values.
Results may differ from the reference program's by a relative error of at most 0.012.
Values may be sent and summed in bfloat16 or wider, within the bound.
No kernel may reach another device: no remote copies, remote signals or barrier semaphores. Data moves between devices by JAX's collectives and lax.ppermute only.
A program may use at most 64 MiB of HBM per device.

```python
import jax
import jax.numpy as jnp
from jax import lax

D = 512
NODE_DEV = 128
EDGE_DEV = 2048
REACH = 2
NEAR = 48
CAP = 2
LAYERS = 2
PEERS = 16
NODES = 2048
EDGES = 32768


def endpoint_slots(key, salt_value, far_phase, low_position, high_position):
    total = PEERS * EDGE_DEV
    near_rows = (2 * REACH + 1) * NEAR
    position = jnp.arange(total, dtype=jnp.int32) % EDGE_DEV
    offsets = jnp.array([0, 0, 0, 0, -1, 1, -1, 1, -2, 2], dtype=jnp.int32)
    picked = jax.random.randint(jax.random.fold_in(key, salt_value + 1), (total,), 0, 10)
    offset_index = jnp.clip(offsets[picked], -REACH, REACH) + REACH
    near_slot = offset_index * NEAR + jax.random.randint(jax.random.fold_in(key, salt_value + 2), (total,), 0, NEAR)
    far_slot = near_rows + jax.random.randint(jax.random.fold_in(key, salt_value + 3), (total,), 0, PEERS * CAP)
    slots = jnp.where(position % 8 == far_phase, far_slot, near_slot)
    slots = jnp.where(position == low_position, 0, slots)
    slots = jnp.where(position == high_position, near_rows + PEERS * CAP - 1, slots)
    return slots.astype(jnp.int32)


def draw_near_table(key, part):
    picked = jax.random.randint(jax.random.fold_in(key, 5), (PEERS, 2 * REACH + 1, NEAR), 0, NODE_DEV)
    picked = picked.at[0, 0, 0].set(0)
    picked = picked.at[PEERS - 1, 2 * REACH, NEAR - 1].set(NODE_DEV - 1)
    return picked.astype(jnp.int32)


def draw_far_table(key, part):
    picked = jax.random.randint(jax.random.fold_in(key, 7), (PEERS, PEERS, CAP), 0, NODE_DEV)
    picked = picked.at[0, 0, 0].set(0)
    picked = picked.at[PEERS - 1, PEERS - 1, CAP - 1].set(NODE_DEV - 1)
    return picked.astype(jnp.int32)


def draw_edge_sender(key, part):
    return endpoint_slots(key, 20, 0, 1, EDGE_DEV - 1)


def draw_edge_receiver(key, part):
    return endpoint_slots(key, 40, 4, 2, EDGE_DEV - 2)


def level_of(key, extent, split, low, largest):
    factor_of, own = 1.0, jax.random.fold_in(key, 6)
    for dim, parts in split:
        steps = jnp.exp(jax.random.uniform(jax.random.fold_in(own, dim), (parts,), jnp.float32, low / len(split), largest / len(split)))
        factor_of = factor_of * jnp.repeat(steps, extent[dim] // parts).reshape([-1 if axis == dim else 1 for axis in range(len(extent))])
    return factor_of


def noise(own_key, dims, width, limit, shards=(), held_as=jnp.bfloat16):
    result = width * jax.random.normal(own_key, dims, jnp.float32)
    if shards:
        result = result * level_of(own_key, dims, shards, -0.22, 0.18)
    return jnp.clip(result, -limit, limit).astype(held_as)


def setup_inputs(seed: int = 0, part: int = 0) -> dict:
    seeds = jax.random.split(jax.random.key(seed), 17)
    own_keys = jax.random.split(jax.random.fold_in(seeds[16], part), 17)
    nodes = noise(own_keys[0], (NODES, D), 1.0, 6.0, ((0, 16),))
    edges = noise(own_keys[1], (EDGES, D), 1.0, 6.0, ((0, 16),))
    near_table = draw_near_table(jax.random.fold_in(jax.random.fold_in(seeds[16], part), 71), part)
    far_table = draw_far_table(jax.random.fold_in(jax.random.fold_in(seeds[16], part), 71), part)
    edge_sender = draw_edge_sender(jax.random.fold_in(jax.random.fold_in(seeds[16], part), 71), part)
    edge_receiver = draw_edge_receiver(jax.random.fold_in(jax.random.fold_in(seeds[16], part), 71), part)
    edge_w1 = noise(seeds[6], (LAYERS, 3 * D, D), (3 * D) ** -0.5, 0.15625)
    edge_b1 = noise(seeds[7], (LAYERS, D), 1.0, 4.0, (), jnp.float32)
    edge_w2 = noise(seeds[8], (LAYERS, D, D), D ** -0.5, 0.25)
    edge_gain = jnp.clip(jax.random.uniform(seeds[9], (LAYERS, D), jnp.float32, 0.5, 1.5), 0.5, 1.5)
    edge_shift = noise(seeds[10], (LAYERS, D), 0.5, 3.0, (), jnp.float32)
    node_w1 = noise(seeds[11], (LAYERS, 2 * D, D), (2 * D) ** -0.5, 0.1875)
    node_b1 = noise(seeds[12], (LAYERS, D), 1.0, 4.0, (), jnp.float32)
    node_w2 = noise(seeds[13], (LAYERS, D, D), D ** -0.5, 0.25)
    node_gain = jnp.clip(jax.random.uniform(seeds[14], (LAYERS, D), jnp.float32, 0.5, 1.5), 0.5, 1.5)
    node_shift = noise(seeds[15], (LAYERS, D), 0.5, 3.0, (), jnp.float32)
    return {"nodes": nodes, "edges": edges, "near_table": near_table, "far_table": far_table, "edge_sender": edge_sender, "edge_receiver": edge_receiver, "edge_w1": edge_w1, "edge_b1": edge_b1, "edge_w2": edge_w2, "edge_gain": edge_gain, "edge_shift": edge_shift, "node_w1": node_w1, "node_b1": node_b1, "node_w2": node_w2, "node_gain": node_gain, "node_shift": node_shift}


EPSILON = 1e-05

def layer_norm(values, norm_gain, norm_shift):
    center = values - lax.optimization_barrier(jnp.mean(values, axis=-1, keepdims=True))
    spread = lax.optimization_barrier(jnp.mean(center * center, axis=-1, keepdims=True))
    return center * lax.rsqrt(spread + EPSILON) * norm_gain + norm_shift

def finish(old_state, mixed_rows, norm_gain, norm_shift):
    return (old_state.astype(jnp.float32) + layer_norm(mixed_rows, norm_gain, norm_shift)).astype(jnp.bfloat16)

def two_layer(joined, first_weight, bias_row, second_weight):
    pre_act = jnp.dot(joined, first_weight, preferred_element_type=jnp.float32)
    hidden = jax.nn.silu(pre_act + bias_row).astype(jnp.bfloat16)
    return jnp.dot(hidden, second_weight, preferred_element_type=jnp.float32)

def reference(nodes, edges, near_table, far_table, edge_sender, edge_receiver, edge_w1, edge_b1, edge_w2, edge_gain, edge_shift, node_w1, node_b1, node_w2, node_gain, node_shift):
    holder = (jnp.arange(EDGES, dtype=jnp.int32) // EDGE_DEV).astype(jnp.int32)
    near_rows = (2 * REACH + 1) * NEAR

    def global_ids(slots):
        is_near = slots < near_rows
        offset_index = jnp.minimum(slots // NEAR, 2 * REACH).astype(jnp.int32)
        near_slot = (slots % NEAR).astype(jnp.int32)
        near_source = ((holder - (offset_index - REACH)) % PEERS).astype(jnp.int32)
        near_ids = near_source * NODE_DEV + near_table[near_source, offset_index, near_slot]
        far_index = jnp.maximum(slots - near_rows, 0).astype(jnp.int32)
        far_source = (far_index // CAP).astype(jnp.int32)
        far_slot = (far_index % CAP).astype(jnp.int32)
        far_ids = far_source * NODE_DEV + far_table[far_source, holder, far_slot]
        return jnp.where(is_near, near_ids, far_ids).astype(jnp.int32)
    sender_ids = global_ids(edge_sender)
    receiver_ids = global_ids(edge_receiver)
    states = nodes
    edge_state = edges
    for layer_index in range(LAYERS):

        def update_block(packed):
            block_edges, block_send, block_recv = packed
            joined = jnp.concatenate([block_edges, states[block_send], states[block_recv]], axis=1)
            mixed_rows = two_layer(joined, edge_w1[layer_index], edge_b1[layer_index], edge_w2[layer_index])
            return finish(block_edges, mixed_rows, edge_gain[layer_index], edge_shift[layer_index])
        edge_state = lax.map(update_block, (edge_state.reshape(PEERS, EDGE_DEV, D), sender_ids.reshape(PEERS, EDGE_DEV), receiver_ids.reshape(PEERS, EDGE_DEV))).reshape(EDGES, D)
        aggregate = jax.ops.segment_sum(edge_state.astype(jnp.float32), receiver_ids, num_segments=NODES)
        joined_nodes = jnp.concatenate([states, aggregate.astype(jnp.bfloat16)], axis=1)
        node_mixed = two_layer(joined_nodes, node_w1[layer_index], node_b1[layer_index], node_w2[layer_index])
        states = finish(states, node_mixed, node_gain[layer_index], node_shift[layer_index])
    return (states, edge_state)
```

```python
import functools

import jax
import jax.numpy as jnp
from jax import lax
from jax.experimental import pallas as pl
from jax.experimental.pallas import tpu as pltpu
from jax.sharding import PartitionSpec as P

EPSILON = 1e-05
PEERS = ("node", "feat")
ROWS = 256
LANES = 128


def passed_along(block, distance):
    count = lax.axis_size(PEERS)
    route = [((i - distance) % count, i) for i in range(count)]
    return lax.ppermute(block, PEERS, route)


def exchange_far(block):
    return lax.all_to_all(block, PEERS, split_axis=0, concat_axis=0, tiled=True)


def dot(left, right):
    return jnp.dot(left, right, preferred_element_type=jnp.float32)


def dot_rows(left, right):
    return lax.dot_general(
        left, right, (((0,), (0,)), ((), ())), preferred_element_type=jnp.float32
    )


def silu(values):
    half = 0.5 * values
    return half * jnp.tanh(half) + half


def layer_norm(values, norm_gain, norm_shift):
    center = values - jnp.mean(values, axis=-1, keepdims=True)
    spread = jnp.mean(center * center, axis=-1, keepdims=True)
    return center * lax.rsqrt(spread + EPSILON) * norm_gain + norm_shift


def iota(shape, axis):
    return lax.broadcasted_iota(jnp.int32, shape, axis)


def hot(left, right):
    return jnp.where(left == right, 1.0, 0.0).astype(jnp.bfloat16)


def far_rows(far_ref):
    table = far_ref[0].astype(jnp.float32)
    peers, width = table.shape
    total = peers * width
    spread = jnp.where(iota((total, peers), 0) // width == iota((total, peers), 1), 1.0, 0.0)
    wide = jnp.dot(
        spread, table, preferred_element_type=jnp.float32, precision=lax.Precision.HIGHEST
    )
    own = iota((total, width), 0) % width == iota((total, width), 1)
    return jnp.sum(jnp.where(own, wide, 0.0), axis=1, keepdims=True).astype(jnp.int32)


def place(states, near_ref, far_ref, near_outs, far_out):
    rows = states.shape[0]
    width = near_ref.shape[2]
    for k, out in enumerate(near_outs):
        picks = hot(iota((rows, width), 0), near_ref[0, k : k + 1, :])
        out[...] = dot_rows(picks, states).astype(out.dtype)
    peers, slots = far_ref.shape[1:]
    chosen = far_rows(far_ref)
    picks = hot(iota((peers * slots, rows), 1), chosen)
    found = dot(picks, states)
    for q in range(peers):
        far_out[q] = found[q * slots : (q + 1) * slots, :].astype(far_out.dtype)


def place_kernel(span, nodes, near, far, *outs):
    place(nodes[...], near, far, outs[:span], outs[span])


def prep_kernel(layer, slots, sender, receiver, edges, w1, b1, hot_out, hot_flip, start_out):
    rows = edges.shape[0]
    width = hot_out.shape[1]
    step = pl.program_id(0)
    for part in range(rows // LANES):
        lane = pl.ds(part * LANES, LANES)
        index = step * (rows // LANES) + part
        s = sender[pl.ds(index, 1), :]
        r = receiver[pl.ds(index, 1), :]
        hot_s = jnp.where(iota((slots, LANES), 0) == s, 1.0, 0.0)
        hot_r = jnp.where(iota((slots, LANES), 0) == r, 1.0, 0.0)
        hot_flip[:, part * LANES : (part + 1) * LANES] = hot_r.astype(jnp.bfloat16)
        pad = jnp.zeros((width - 2 * slots, LANES), jnp.float32)
        both = jnp.concatenate([hot_s, hot_r, pad], axis=0)
        hot_out[lane, :] = both.T.astype(jnp.bfloat16)
    start = dot(edges[...], w1[0]) + b1[layer : layer + 1, :]
    start_out[...] = start.astype(start_out.dtype)


def start_kernel(layer, edges, w1, b1, start_out):
    start = dot(edges[...], w1[0]) + b1[layer : layer + 1, :]
    start_out[...] = start.astype(start_out.dtype)


def edge_kernel(layer, span, hot_in, hot_flip, start, edges, *refs):
    near_in, refs = refs[:span], refs[span:]
    far_in, w1s, w1r, w2, gain, shift = refs[:6]
    edge_out, refs = refs[6], refs[7:]
    near_out, far_out = refs[:span], refs[span]
    arrived, table, total = refs[span + 1 :]
    step = pl.program_id(0)
    slots = hot_flip.shape[0]
    near_width = near_in[0].shape[0]
    near_total = span * near_width
    peers, width = far_in.shape[:2]

    @pl.when(step == 0)
    def _():
        for k in range(span):
            arrived[k * near_width : (k + 1) * near_width, :] = near_in[k][...].astype(jnp.float32)
        for q in range(peers):
            low = near_total + q * width
            arrived[low : low + width, :] = far_in[q].astype(jnp.float32)
        here = arrived[...].astype(jnp.bfloat16)
        table[0:slots, :] = dot(here, w1s[0]).astype(jnp.bfloat16)
        table[slots : 2 * slots, :] = dot(here, w1r[0]).astype(jnp.bfloat16)
        rest = table.shape[0] - 2 * slots
        table[2 * slots :, :] = jnp.zeros((rest, table.shape[1]), jnp.bfloat16)
        total[...] = jnp.zeros_like(total)

    pre = dot(hot_in[...], table[...]) + start[...].astype(jnp.float32)
    hidden = silu(pre).astype(jnp.bfloat16)
    mixed = dot(hidden, w2[0])
    normed = layer_norm(mixed, gain[layer : layer + 1, :], shift[layer : layer + 1, :])
    fresh = (edges[...].astype(jnp.float32) + normed).astype(jnp.bfloat16)
    edge_out[...] = fresh
    total[...] += dot(hot_flip[...], fresh)

    @pl.when(step == pl.num_programs(0) - 1)
    def _():
        for k in range(span):
            near_out[k][...] = total[k * near_width : (k + 1) * near_width, :].astype(jnp.bfloat16)
        for q in range(peers):
            low = near_total + q * width
            far_out[q] = total[low : low + width, :].astype(jnp.bfloat16)


def node_kernel(layer, span, last, nodes, near, far, *refs):
    near_in, refs = refs[:span], refs[span:]
    far_in, w1, b1, w2, gain, shift = refs[:6]
    node_out, refs = refs[6], refs[7:]
    far_back = refs[-1]
    states = nodes[...]
    rows = states.shape[0]
    near_width = near.shape[2]
    peers, width = far_in.shape[:2]
    summed = jnp.zeros(states.shape, jnp.float32)
    for k in range(span):
        picks = hot(iota((rows, near_width), 0), near[0, k : k + 1, :])
        summed += dot(picks, near_in[k][...])
    for q in range(peers):
        far_back[q * width : (q + 1) * width, :] = far_in[q].astype(jnp.float32)
    picks = hot(iota((peers * width, rows), 1), far_rows(far))
    summed += dot_rows(picks, far_back[...].astype(jnp.bfloat16))
    features = states.shape[1]
    pre = dot(states, w1[0, :features, :])
    pre += dot(summed.astype(jnp.bfloat16), w1[0, features:, :])
    hidden = silu(pre + b1[layer : layer + 1, :]).astype(jnp.bfloat16)
    mixed = dot(hidden, w2[0])
    normed = layer_norm(mixed, gain[layer : layer + 1, :], shift[layer : layer + 1, :])
    fresh = (states.astype(jnp.float32) + normed).astype(jnp.bfloat16)
    node_out[...] = fresh
    if not last:
        place(fresh, near, far, refs[:span], refs[span])


def whole(shape):
    return pl.BlockSpec(shape, lambda *_: (0,) * len(shape))


def cost(flops, moved):
    return pl.CostEstimate(flops=flops, bytes_accessed=moved, transcendentals=0)


def params(limit):
    return pltpu.CompilerParams(vmem_limit_bytes=limit << 20)


def on_device(
    nodes,
    edges,
    near_table,
    far_table,
    edge_sender,
    edge_receiver,
    edge_w1,
    edge_b1,
    edge_w2,
    edge_gain,
    edge_shift,
    node_w1,
    node_b1,
    node_w2,
    node_gain,
    node_shift,
):
    span, near_width = near_table.shape[1:]
    reach = (span - 1) // 2
    peers, far_width = far_table.shape[1:]
    slots = span * near_width + peers * far_width
    node_rows, features = nodes.shape
    edge_rows = edges.shape[0]
    layers = edge_w1.shape[0]
    steps = edge_rows // ROWS
    hot_width = -(-2 * slots // LANES) * LANES
    narrow = jnp.bfloat16
    near_shape = jax.ShapeDtypeStruct((near_width, features), narrow)
    far_shape = jax.ShapeDtypeStruct((peers, far_width, features), narrow)
    sent_shapes = [near_shape] * span + [far_shape]
    edge_shape = jax.ShapeDtypeStruct(edges.shape, narrow)
    sent_specs = [whole(near_shape.shape)] * span + [whole(far_shape.shape)]
    by_rows = pl.BlockSpec((ROWS, features), lambda i: (i, 0))
    vector_spec = whole(edge_b1.shape)

    def weight(layer, block, depth):
        return pl.BlockSpec((1, depth, features), lambda *_: (layer, block, 0))

    def move(sent, sign):
        *near, far = sent
        far = exchange_far(far)
        back = []
        for k in range(span):
            offset = sign * (k - reach)
            back.append(near[k] if offset == 0 else passed_along(near[k], offset))
        return back + [far]

    sent = pl.pallas_call(
        functools.partial(place_kernel, span),
        out_shape=sent_shapes,
        in_specs=[whole(nodes.shape), whole(near_table.shape), whole(far_table.shape)],
        out_specs=sent_specs,
        grid=(1,),
        compiler_params=params(16),
        cost_estimate=cost(2 * slots * node_rows * features, 2 * slots * features * 2),
        name="place",
    )(nodes, near_table, far_table)
    sender = edge_sender.reshape(edge_rows // LANES, LANES)
    receiver = edge_receiver.reshape(edge_rows // LANES, LANES)
    hot_rows, hot_flip, start = pl.pallas_call(
        functools.partial(prep_kernel, 0, slots),
        out_shape=[
            jax.ShapeDtypeStruct((edge_rows, hot_width), narrow),
            jax.ShapeDtypeStruct((slots, edge_rows), narrow),
            edge_shape,
        ],
        grid=(steps,),
        in_specs=[
            whole(sender.shape),
            whole(receiver.shape),
            by_rows,
            weight(0, 0, features),
            vector_spec,
        ],
        out_specs=[
            pl.BlockSpec((ROWS, hot_width), lambda i: (i, 0)),
            pl.BlockSpec((slots, ROWS), lambda i: (0, i)),
            by_rows,
        ],
        compiler_params=params(24),
        cost_estimate=cost(2 * edge_rows * features * features, 8 * edge_rows * features),
        name="prep",
    )(sender, receiver, edges, edge_w1, edge_b1)

    states = nodes
    edge_state = edges
    for layer in range(layers):
        last = layer == layers - 1
        arrived = move(sent, 1)
        if layer > 0:
            start = pl.pallas_call(
                functools.partial(start_kernel, layer),
                out_shape=edge_shape,
                grid=(steps,),
                in_specs=[by_rows, weight(layer, 0, features), vector_spec],
                out_specs=by_rows,
                compiler_params=params(16),
                cost_estimate=cost(2 * edge_rows * features * features, 4 * edge_rows * features),
                name="start",
            )(edge_state, edge_w1, edge_b1)
        edge_state, *sums = pl.pallas_call(
            functools.partial(edge_kernel, layer, span),
            out_shape=[edge_shape] + sent_shapes,
            grid=(steps,),
            in_specs=[
                pl.BlockSpec((ROWS, hot_width), lambda i: (i, 0)),
                pl.BlockSpec((slots, ROWS), lambda i: (0, i)),
                by_rows,
                by_rows,
            ]
            + sent_specs
            + [
                weight(layer, 1, features),
                weight(layer, 2, features),
                weight(layer, 0, features),
                vector_spec,
                vector_spec,
            ],
            out_specs=[by_rows] + sent_specs,
            scratch_shapes=[
                pltpu.VMEM((slots, features), jnp.float32),
                pltpu.VMEM((hot_width, features), narrow),
                pltpu.VMEM((slots, features), jnp.float32),
            ],
            compiler_params=params(32),
            cost_estimate=cost(
                2 * edge_rows * features * (hot_width + features + slots),
                10 * edge_rows * features,
            ),
            name="edge",
        )(
            hot_rows,
            hot_flip,
            start,
            edge_state,
            *arrived,
            edge_w1,
            edge_w1,
            edge_w2,
            edge_gain,
            edge_shift,
        )
        returned = move(sums, -1)
        outs = pl.pallas_call(
            functools.partial(node_kernel, layer, span, last),
            out_shape=[jax.ShapeDtypeStruct(nodes.shape, narrow)] + ([] if last else sent_shapes),
            grid=(1,),
            in_specs=[whole(nodes.shape), whole(near_table.shape), whole(far_table.shape)]
            + sent_specs
            + [
                weight(layer, 0, 2 * features),
                vector_spec,
                weight(layer, 0, features),
                vector_spec,
                vector_spec,
            ],
            out_specs=[whole(nodes.shape)] + ([] if last else sent_specs),
            scratch_shapes=[pltpu.VMEM((peers * far_width, features), jnp.float32)],
            compiler_params=params(16),
            cost_estimate=cost(6 * node_rows * features * features, 6 * features * features),
            name="node",
        )(
            states,
            near_table,
            far_table,
            *returned,
            node_w1,
            node_b1,
            node_w2,
            node_gain,
            node_shift,
        )
        states, sent = outs[0], outs[1:]
    return (states, edge_state)


def solution(mesh):
    split = ("ens", "node", "feat")
    return jax.shard_map(
        on_device,
        mesh=mesh,
        in_specs=(
            P(split, None),
            P(split, None),
            P(split, None, None),
            P(split, None, None),
            P(split),
            P(split),
        )
        + (P(),) * 10,
        out_specs=(P(split, None), P(split, None)),
        check_vma=False,
    )
```

```python
import functools

import jax
import jax.numpy as jnp
from jax import lax
from jax.experimental import pallas as pl
from jax.experimental.pallas import tpu as pltpu
from jax.sharding import PartitionSpec as P

EPSILON = 1e-05
PEERS = ("node", "feat")
ROWS = 256
LANES = 128


def passed_along(block, distance):
    count = lax.axis_size(PEERS)
    route = [((i - distance) % count, i) for i in range(count)]
    return lax.ppermute(block, PEERS, route)


def exchange_far(block):
    return lax.all_to_all(block, PEERS, split_axis=0, concat_axis=0, tiled=True)


def dot(left, right):
    return jnp.dot(left, right, preferred_element_type=jnp.float32)


def dot_rows(left, right):
    return lax.dot_general(
        left, right, (((0,), (0,)), ((), ())), preferred_element_type=jnp.float32
    )


def silu(values):
    half = 0.5 * values
    return half * jnp.tanh(half) + half


def layer_norm(values, norm_gain, norm_shift):
    center = values - jnp.mean(values, axis=-1, keepdims=True)
    spread = jnp.mean(center * center, axis=-1, keepdims=True)
    return center * lax.rsqrt(spread + EPSILON) * norm_gain + norm_shift


def iota(shape, axis):
    return lax.broadcasted_iota(jnp.int32, shape, axis)


def hot(left, right):
    return jnp.where(left == right, 1.0, 0.0).astype(jnp.bfloat16)


def far_rows(far_ref):
    table = far_ref[0].astype(jnp.float32)
    width, peers = table.shape
    total = peers * width
    spread = jnp.where(iota((total, peers), 0) // width == iota((total, peers), 1), 1.0, 0.0)
    wide = lax.dot_general(
        spread,
        table,
        (((1,), (1,)), ((), ())),
        preferred_element_type=jnp.float32,
        precision=lax.Precision.HIGHEST,
    )
    own = iota((total, width), 0) % width == iota((total, width), 1)
    return jnp.sum(jnp.where(own, wide, 0.0), axis=1, keepdims=True).astype(jnp.int32)


def place(states, near_ref, far_ref, near_outs, far_out):
    rows = states.shape[0]
    width = near_ref.shape[2]
    for k, out in enumerate(near_outs):
        picks = hot(iota((rows, width), 0), near_ref[k])
        out[...] = dot_rows(picks, states).astype(out.dtype)
    slots, peers = far_ref.shape[1:]
    chosen = far_rows(far_ref)
    picks = hot(iota((peers * slots, rows), 1), chosen)
    found = dot(picks, states)
    for q in range(peers):
        far_out[q] = found[q * slots : (q + 1) * slots, :].astype(far_out.dtype)


def place_kernel(span, nodes, near, far, *outs):
    place(nodes[...], near, far, outs[:span], outs[span])


def prep_kernel(layer, slots, sender, receiver, edges, w1, b1, hot_out, hot_flip, start_out):
    rows = edges.shape[0]
    width = hot_out.shape[1]
    step = pl.program_id(0)
    for part in range(rows // LANES):
        lane = pl.ds(part * LANES, LANES)
        index = step * (rows // LANES) + part
        s = sender[pl.ds(index, 1), :]
        r = receiver[pl.ds(index, 1), :]
        hot_s = jnp.where(iota((slots, LANES), 0) == s, 1.0, 0.0)
        hot_r = jnp.where(iota((slots, LANES), 0) == r, 1.0, 0.0)
        hot_flip[:, part * LANES : (part + 1) * LANES] = hot_r.astype(jnp.bfloat16)
        pad = jnp.zeros((width - 2 * slots, LANES), jnp.float32)
        both = jnp.concatenate([hot_s, hot_r, pad], axis=0)
        hot_out[lane, :] = both.T.astype(jnp.bfloat16)
    start = dot(edges[...], w1[0]) + b1[layer : layer + 1, :]
    start_out[...] = start.astype(start_out.dtype)


def start_kernel(layer, edges, w1, b1, start_out):
    start = dot(edges[...], w1[0]) + b1[layer : layer + 1, :]
    start_out[...] = start.astype(start_out.dtype)


def edge_kernel(layer, span, hot_in, hot_flip, start, edges, *refs):
    near_in, refs = refs[:span], refs[span:]
    far_in, w1s, w1r, w2, gain, shift = refs[:6]
    edge_out, refs = refs[6], refs[7:]
    near_out, far_out = refs[:span], refs[span]
    arrived, table, total = refs[span + 1 :]
    step = pl.program_id(0)
    slots = hot_flip.shape[0]
    near_width = near_in[0].shape[0]
    near_total = span * near_width
    peers, width = far_in.shape[:2]

    @pl.when(step == 0)
    def _():
        for k in range(span):
            arrived[k * near_width : (k + 1) * near_width, :] = near_in[k][...].astype(jnp.float32)
        for q in range(peers):
            low = near_total + q * width
            arrived[low : low + width, :] = far_in[q].astype(jnp.float32)
        here = arrived[...].astype(jnp.bfloat16)
        table[0:slots, :] = dot(here, w1s[0]).astype(jnp.bfloat16)
        table[slots : 2 * slots, :] = dot(here, w1r[0]).astype(jnp.bfloat16)
        rest = table.shape[0] - 2 * slots
        table[2 * slots :, :] = jnp.zeros((rest, table.shape[1]), jnp.bfloat16)
        total[...] = jnp.zeros_like(total)

    pre = dot(hot_in[...], table[...]) + start[...].astype(jnp.float32)
    hidden = silu(pre).astype(jnp.bfloat16)
    mixed = dot(hidden, w2[0])
    normed = layer_norm(mixed, gain[layer : layer + 1, :], shift[layer : layer + 1, :])
    fresh = (edges[...].astype(jnp.float32) + normed).astype(jnp.bfloat16)
    edge_out[...] = fresh
    total[...] += dot(hot_flip[...], fresh)

    @pl.when(step == pl.num_programs(0) - 1)
    def _():
        for k in range(span):
            near_out[k][...] = total[k * near_width : (k + 1) * near_width, :].astype(jnp.bfloat16)
        for q in range(peers):
            low = near_total + q * width
            far_out[q] = total[low : low + width, :].astype(jnp.bfloat16)


def node_kernel(layer, span, last, nodes, near, far, *refs):
    near_in, refs = refs[:span], refs[span:]
    far_in, w1, b1, w2, gain, shift = refs[:6]
    node_out, refs = refs[6], refs[7:]
    far_back = refs[-1]
    states = nodes[...]
    rows = states.shape[0]
    near_width = near.shape[2]
    peers, width = far_in.shape[:2]
    summed = jnp.zeros(states.shape, jnp.float32)
    for k in range(span):
        picks = hot(iota((rows, near_width), 0), near[k])
        summed += dot(picks, near_in[k][...])
    for q in range(peers):
        far_back[q * width : (q + 1) * width, :] = far_in[q].astype(jnp.float32)
    picks = hot(iota((peers * width, rows), 1), far_rows(far))
    summed += dot_rows(picks, far_back[...].astype(jnp.bfloat16))
    features = states.shape[1]
    pre = dot(states, w1[0, :features, :])
    pre += dot(summed.astype(jnp.bfloat16), w1[0, features:, :])
    hidden = silu(pre + b1[layer : layer + 1, :]).astype(jnp.bfloat16)
    mixed = dot(hidden, w2[0])
    normed = layer_norm(mixed, gain[layer : layer + 1, :], shift[layer : layer + 1, :])
    fresh = (states.astype(jnp.float32) + normed).astype(jnp.bfloat16)
    node_out[...] = fresh
    if not last:
        place(fresh, near, far, refs[:span], refs[span])


def stay(array):
    return pltpu.with_memory_space_constraint(array, pltpu.HBM)


def whole(shape):
    return pl.BlockSpec(shape, lambda *_: (0,) * len(shape))


def cost(flops, moved):
    return pl.CostEstimate(flops=flops, bytes_accessed=moved, transcendentals=0)


def params(limit):
    return pltpu.CompilerParams(vmem_limit_bytes=limit << 20)


def on_device(
    nodes,
    edges,
    near_table,
    far_table,
    edge_sender,
    edge_receiver,
    edge_w1,
    edge_b1,
    edge_w2,
    edge_gain,
    edge_shift,
    node_w1,
    node_b1,
    node_w2,
    node_gain,
    node_shift,
):
    span, near_width = near_table.shape[1:]
    reach = (span - 1) // 2
    peers, far_width = far_table.shape[1:]
    slots = span * near_width + peers * far_width
    node_rows, features = nodes.shape
    edge_rows = edges.shape[0]
    layers = edge_w1.shape[0]
    steps = edge_rows // ROWS
    hot_width = -(-2 * slots // LANES) * LANES
    narrow = jnp.bfloat16
    near_table = stay(near_table.transpose(1, 0, 2))
    far_table = stay(far_table.transpose(0, 2, 1))
    nodes, edges, edge_w1, edge_w2 = map(stay, (nodes, edges, edge_w1, edge_w2))
    edge_b1, edge_gain, edge_shift = map(stay, (edge_b1, edge_gain, edge_shift))
    node_w1, node_w2 = map(stay, (node_w1, node_w2))
    node_b1, node_gain, node_shift = map(stay, (node_b1, node_gain, node_shift))
    near_shape = jax.ShapeDtypeStruct((near_width, features), narrow)
    far_shape = jax.ShapeDtypeStruct((peers, far_width, features), narrow)
    sent_shapes = [near_shape] * span + [far_shape]
    edge_shape = pltpu.HBM(edges.shape, narrow)
    sent_specs = [whole(near_shape.shape)] * span + [whole(far_shape.shape)]
    by_rows = pl.BlockSpec((ROWS, features), lambda i: (i, 0))
    vector_spec = whole(edge_b1.shape)

    def weight(layer, block, depth):
        return pl.BlockSpec((1, depth, features), lambda *_: (layer, block, 0))

    def move(sent, sign):
        *near, far = sent
        far = exchange_far(far)
        back = []
        for k in range(span):
            offset = sign * (k - reach)
            back.append(near[k] if offset == 0 else passed_along(near[k], offset))
        return back + [far]

    sent = pl.pallas_call(
        functools.partial(place_kernel, span),
        out_shape=sent_shapes,
        in_specs=[whole(nodes.shape), whole(near_table.shape), whole(far_table.shape)],
        out_specs=sent_specs,
        grid=(1,),
        compiler_params=params(24),
        cost_estimate=cost(2 * slots * node_rows * features, 2 * slots * features * 2),
        name="place",
    )(nodes, near_table, far_table)
    sender = stay(edge_sender.reshape(edge_rows // LANES, LANES))
    receiver = stay(edge_receiver.reshape(edge_rows // LANES, LANES))
    hot_rows, hot_flip, start = pl.pallas_call(
        functools.partial(prep_kernel, 0, slots),
        out_shape=[
            pltpu.HBM((edge_rows, hot_width), narrow),
            pltpu.HBM((slots, edge_rows), narrow),
            edge_shape,
        ],
        grid=(steps,),
        in_specs=[
            whole(sender.shape),
            whole(receiver.shape),
            by_rows,
            weight(0, 0, features),
            vector_spec,
        ],
        out_specs=[
            pl.BlockSpec((ROWS, hot_width), lambda i: (i, 0)),
            pl.BlockSpec((slots, ROWS), lambda i: (0, i)),
            by_rows,
        ],
        compiler_params=params(24),
        cost_estimate=cost(2 * edge_rows * features * features, 8 * edge_rows * features),
        name="prep",
    )(sender, receiver, edges, edge_w1, edge_b1)

    states = nodes
    edge_state = edges
    for layer in range(layers):
        last = layer == layers - 1
        arrived = move(sent, 1)
        if layer > 0:
            start = pl.pallas_call(
                functools.partial(start_kernel, layer),
                out_shape=edge_shape,
                grid=(steps,),
                in_specs=[by_rows, weight(layer, 0, features), vector_spec],
                out_specs=by_rows,
                compiler_params=params(24),
                cost_estimate=cost(2 * edge_rows * features * features, 4 * edge_rows * features),
                name="start",
            )(stay(edge_state), edge_w1, edge_b1)
        edge_state, *sums = pl.pallas_call(
            functools.partial(edge_kernel, layer, span),
            out_shape=[edge_shape] + sent_shapes,
            grid=(steps,),
            in_specs=[
                pl.BlockSpec((ROWS, hot_width), lambda i: (i, 0)),
                pl.BlockSpec((slots, ROWS), lambda i: (0, i)),
                by_rows,
                by_rows,
            ]
            + sent_specs
            + [
                weight(layer, 1, features),
                weight(layer, 2, features),
                weight(layer, 0, features),
                vector_spec,
                vector_spec,
            ],
            out_specs=[by_rows] + sent_specs,
            scratch_shapes=[
                pltpu.VMEM((slots, features), jnp.float32),
                pltpu.VMEM((hot_width, features), narrow),
                pltpu.VMEM((slots, features), jnp.float32),
            ],
            compiler_params=params(24),
            cost_estimate=cost(
                2 * edge_rows * features * (hot_width + features + slots),
                10 * edge_rows * features,
            ),
            name="edge",
        )(
            stay(hot_rows),
            stay(hot_flip),
            stay(start),
            stay(edge_state),
            *arrived,
            edge_w1,
            edge_w1,
            edge_w2,
            edge_gain,
            edge_shift,
        )
        returned = move(sums, -1)
        outs = pl.pallas_call(
            functools.partial(node_kernel, layer, span, last),
            out_shape=[jax.ShapeDtypeStruct(nodes.shape, narrow)] + ([] if last else sent_shapes),
            grid=(1,),
            in_specs=[whole(nodes.shape), whole(near_table.shape), whole(far_table.shape)]
            + sent_specs
            + [
                weight(layer, 0, 2 * features),
                vector_spec,
                weight(layer, 0, features),
                vector_spec,
                vector_spec,
            ],
            out_specs=[whole(nodes.shape)] + ([] if last else sent_specs),
            scratch_shapes=[pltpu.VMEM((peers * far_width, features), jnp.float32)],
            compiler_params=params(24),
            cost_estimate=cost(6 * node_rows * features * features, 6 * features * features),
            name="node",
        )(
            states,
            near_table,
            far_table,
            *returned,
            node_w1,
            node_b1,
            node_w2,
            node_gain,
            node_shift,
        )
        states, sent = outs[0], outs[1:]
    return (states, edge_state)


def solution(mesh):
    split = ("ens", "node", "feat")
    return jax.shard_map(
        on_device,
        mesh=mesh,
        in_specs=(
            P(split, None),
            P(split, None),
            P(split, None, None),
            P(split, None, None),
            P(split),
            P(split),
        )
        + (P(),) * 10,
        out_specs=(P(split, None), P(split, None)),
        check_vma=False,
    )
```

```python
import functools

import jax
import jax.numpy as jnp
from jax import lax
from jax.experimental import pallas as pl
from jax.experimental.pallas import tpu as pltpu
from jax.sharding import PartitionSpec as P

EPSILON = 1e-05
PEERS = ("node", "feat")
ROWS = 256
LANES = 128
NARROW = jnp.bfloat16


def grid_size():
    return lax.axis_size("node"), lax.axis_size("feat")


def side(column, columns):
    return 1 if column >= columns // 2 else -1


def along_node(block, distance):
    lines, columns = grid_size()
    route = []
    for z in range(lines):
        for f in range(columns):
            target = (z + side(f, columns) * distance) % lines
            route.append((z * columns + f, target * columns + f))
    return lax.ppermute(block, PEERS, route)


def along_feat(block, distance):
    lines, columns = grid_size()
    route = []
    for z in range(lines):
        for f in range(columns):
            route.append((z * columns + f, z * columns + (f + distance) % columns))
    return lax.ppermute(block, PEERS, route)


def dot(left, right):
    return jnp.dot(left, right, preferred_element_type=jnp.float32)


def dot_rows(left, right):
    return lax.dot_general(
        left, right, (((0,), (0,)), ((), ())), preferred_element_type=jnp.float32
    )


def silu(values):
    half = 0.5 * values
    return half * jnp.tanh(half) + half


def layer_norm(values, norm_gain, norm_shift):
    center = values - jnp.mean(values, axis=-1, keepdims=True)
    spread = jnp.mean(center * center, axis=-1, keepdims=True)
    return center * lax.rsqrt(spread + EPSILON) * norm_gain + norm_shift


def iota(shape, axis):
    return lax.broadcasted_iota(jnp.int32, shape, axis)


def hot(left, right):
    return jnp.where(left == right, 1.0, 0.0).astype(NARROW)


class Plan:
    def __init__(self, near_shape, far_shape):
        self.lines, self.columns = grid_size()
        self.span, _, self.near = near_shape
        self.reach = (self.span - 1) // 2
        self.width = far_shape[1]
        self.line_rows = self.columns * self.width
        self.column_rows = self.lines * self.width
        self.near_total = self.span * self.near
        self.far_total = self.lines * self.line_rows
        self.slots = self.near_total + self.far_total
        self.offsets = [o for o in range(-self.reach, self.reach + 1) if o]

    def here(self):
        return lax.axis_index("node"), lax.axis_index("feat")

    def upper(self, column):
        return column >= self.columns // 2

    def leaves(self, column, offset):
        return jnp.logical_or(column + offset < 0, column + offset >= self.columns)

    def near_in(self, e):
        return [o for o in self.offsets if o % self.columns == e]

    def line_message(self, a):
        return (self.reach * self.near if a == 1 else 0) + self.line_rows

    def column_message(self, e):
        return len(self.near_in(e)) * self.near + self.column_rows

    def block(self, ref, index):
        return ref[index * self.near : (index + 1) * self.near, :].astype(jnp.float32)

    def tail(self, ref, count):
        rows = ref.shape[0]
        return ref[rows - count : rows, :].astype(jnp.float32)

    def line_outs(self, outs, near, far, column):
        for a, out in enumerate(outs, 1):
            parts = [far[a * self.line_rows : (a + 1) * self.line_rows, :]]
            if a == 1:
                upper = self.upper(column)
                relayed = [
                    jnp.where(upper, near[i], near[-i]) for i in range(1, self.reach + 1)
                ]
                parts = relayed + parts
            out[...] = jnp.concatenate(parts, axis=0).astype(out.dtype)

    def column_outs(self, outs, near, far):
        for e, out in enumerate(outs, 1):
            parts = [near[o] for o in self.near_in(e)]
            parts.append(far[e * self.column_rows : (e + 1) * self.column_rows, :])
            out[...] = jnp.concatenate(parts, axis=0).astype(out.dtype)

    def column_near(self, ins):
        near = {}
        for e, ref in enumerate(ins, 1):
            for i, o in enumerate(self.near_in(e)):
                near[o] = self.block(ref, i)
        return near

    def reorder(self, far, outer):
        total = self.far_total
        inner = total // (outer * self.width)
        row = iota((total, total), 0)
        c, rest = row % self.width, row // self.width
        source = ((rest % outer) * inner + rest // outer) * self.width + c
        return dot(hot(iota((total, total), 1), source), far.astype(NARROW))


def far_rows(plan, far_ref):
    z, f = plan.here()
    table = far_ref[0].astype(jnp.float32)
    width, peers = table.shape
    total = peers * width
    row = iota((total, peers), 0)
    e = (row // width) % plan.columns
    a = row // plan.line_rows
    a = jnp.where(plan.upper(f), a, plan.lines - a)
    peer = ((z + a) % plan.lines) * plan.columns + (f + e) % plan.columns
    spread = jnp.where(peer == iota((total, peers), 1), 1.0, 0.0)
    wide = lax.dot_general(
        spread,
        table,
        (((1,), (1,)), ((), ())),
        preferred_element_type=jnp.float32,
        precision=lax.Precision.HIGHEST,
    )
    own = iota((total, width), 0) % width == iota((total, width), 1)
    return jnp.sum(jnp.where(own, wide, 0.0), axis=1, keepdims=True).astype(jnp.int32)


def place(plan, states, near_ref, picks_far, own_out, line_outs):
    rows = states.shape[0]
    near = {}
    for k in range(plan.span):
        picks = hot(iota((rows, plan.near), 0), near_ref[k])
        near[k - plan.reach] = dot_rows(picks, states)
    far = dot(picks_far, states)
    own = [near[k - plan.reach] for k in range(plan.span)] + [far[: plan.line_rows, :]]
    own_out[...] = jnp.concatenate(own, axis=0).astype(own_out.dtype)
    plan.line_outs(line_outs, near, far, plan.here()[1])


def place_kernel(plan, nodes, near, far, own_out, *line_outs):
    states = nodes[...]
    picks = hot(iota((plan.far_total, states.shape[0]), 1), far_rows(plan, far))
    place(plan, states, near, picks, own_out, line_outs)


def turn_out_kernel(plan, own, *refs):
    line_ins, far_out = refs[: plan.lines - 1], refs[plan.lines - 1]
    column_outs = refs[plan.lines :]
    _, f = plan.here()
    near = {}
    for o in plan.offsets:
        mine = plan.block(own, o + plan.reach)
        near[o] = jnp.where(plan.leaves(f, o), plan.block(line_ins[0], abs(o) - 1), mine)
    far = [plan.tail(ref, plan.line_rows) for ref in (own, *line_ins)]
    far = plan.reorder(jnp.concatenate(far, axis=0), plan.lines)
    far_out[...] = far[: plan.column_rows, :].astype(far_out.dtype)
    plan.column_outs(column_outs, near, far)


def turn_back_kernel(plan, kept, *refs):
    column_ins, near_out = refs[: plan.columns - 1], refs[plan.columns - 1]
    line_outs = refs[plan.columns :]
    _, f = plan.here()
    near = plan.column_near(column_ins)
    near[0] = plan.block(kept, 0)
    far = [plan.tail(ref, plan.column_rows) for ref in (kept, *column_ins)]
    far = plan.reorder(jnp.concatenate(far, axis=0), plan.columns)
    own = [near[k - plan.reach] for k in range(plan.span)] + [far[: plan.line_rows, :]]
    near_out[...] = jnp.concatenate(own, axis=0).astype(near_out.dtype)
    plan.line_outs(line_outs, near, far, f)


def fetch(source, target, sem):
    copy = pltpu.make_async_copy(source, target, sem)
    copy.start()
    return copy


def in_order(plan, slot):
    z, f = plan.here()
    t = jnp.maximum(slot - plan.near_total, 0)
    c, p = t % plan.width, t // plan.width
    line, column = p // plan.columns, p % plan.columns
    e = (f - column + plan.columns) % plan.columns
    away = jnp.where(plan.upper(column), z - line, line - z)
    a = (away + plan.lines) % plan.lines
    renamed = plan.near_total + (e * plan.lines + a) * plan.width + c
    return jnp.where(slot < plan.near_total, slot, renamed)


def prep_kernel(plan, layer, sender, receiver, edges, w1, w2, b1, *refs):
    hot_out, flip_out, start_out, held, w1_out, w2_out, weight, in_sems, w_sems = refs
    slots = plan.slots
    edge_rows, width = hot_out.shape
    features = weight.shape[0]
    first = fetch(w1.at[layer, pl.ds(0, features), :], weight, w_sems.at[0])
    arriving = [
        fetch(
            edges.at[pl.ds(step * ROWS, ROWS), :],
            held.at[pl.ds(step * ROWS, ROWS), :],
            in_sems.at[step],
        )
        for step in range(edge_rows // ROWS)
    ]
    second = fetch(w1.at[layer, pl.ds(features, 2 * features), :], w1_out, w_sems.at[1])
    third = fetch(w2.at[layer], w2_out, w_sems.at[2])
    sent = in_order(plan, sender[...])
    received = in_order(plan, receiver[...])
    for index in range(edge_rows // LANES):
        rows = slice(index * LANES, (index + 1) * LANES)
        hot_s = jnp.where(iota((slots, LANES), 0) == sent[index : index + 1, :], 1.0, 0.0)
        hot_r = jnp.where(iota((slots, LANES), 0) == received[index : index + 1, :], 1.0, 0.0)
        flip_out[:, rows] = hot_r.astype(NARROW)
        pad = jnp.zeros((width - 2 * slots, LANES), jnp.float32)
        both = jnp.concatenate([hot_s, hot_r, pad], axis=0)
        hot_out[rows, :] = both.T.astype(NARROW)
    first.wait()
    for step in range(edge_rows // ROWS):
        arriving[step].wait()
        rows = slice(step * ROWS, (step + 1) * ROWS)
        start = dot(held[rows, :], weight[...]) + b1[layer : layer + 1, :]
        start_out[rows, :] = start.astype(start_out.dtype)
    second.wait()
    third.wait()


def start_kernel(layer, edges, w1, w2, b1, start_out, w1_out, w2_out, weight, w_sems):
    features = weight.shape[0]
    first = fetch(w1.at[layer, pl.ds(0, features), :], weight, w_sems.at[0])
    second = fetch(w1.at[layer, pl.ds(features, 2 * features), :], w1_out, w_sems.at[1])
    third = fetch(w2.at[layer], w2_out, w_sems.at[2])
    first.wait()
    for step in range(edges.shape[0] // ROWS):
        rows = slice(step * ROWS, (step + 1) * ROWS)
        start = dot(edges[rows, :], weight[...]) + b1[layer : layer + 1, :]
        start_out[rows, :] = start.astype(start_out.dtype)
    second.wait()
    third.wait()


def edge_kernel(plan, layer, last, hot_in, flip_in, start_in, edge_in, w1, w2, gain, shift, *refs):
    own, far_first, *refs = refs
    column_ins, refs = refs[: plan.columns - 1], refs[plan.columns - 1 :]
    node_w1, node_w2, edge_out, kept_out, *refs = refs
    column_outs, refs = refs[: plan.columns - 1], refs[plan.columns - 1 :]
    w1_out, w2_out, hidden, table, w_sems, *refs = refs
    steps = edge_in.shape[0] // ROWS
    slots, features = plan.slots, edge_in.shape[1]
    carried = [
        fetch(node_w1.at[layer], w1_out, w_sems.at[0]),
        fetch(node_w2.at[layer], w2_out, w_sems.at[1]),
    ]
    near = plan.column_near(column_ins)
    near[0] = plan.block(own, plan.reach)
    arrived = [near[k - plan.reach] for k in range(plan.span)]
    arrived += [plan.tail(ref, plan.column_rows) for ref in (far_first, *column_ins)]
    arrived = jnp.concatenate(arrived, axis=0).astype(NARROW)
    rest = table.shape[0] - 2 * slots
    table[2 * slots :, :] = jnp.zeros((rest, features), NARROW)
    table[0:slots, :] = dot(arrived, w1[:features, :]).astype(NARROW)
    table[slots : 2 * slots, :] = dot(arrived, w1[features:, :]).astype(NARROW)
    fresh_held = refs[0] if last else edge_out

    def head(step):
        rows = slice(step * ROWS, (step + 1) * ROWS)
        pre = dot(hot_in[rows, :], table[...]) + start_in[rows, :].astype(jnp.float32)
        hidden[step % 2] = silu(pre).astype(NARROW)

    def tail(step):
        rows = slice(step * ROWS, (step + 1) * ROWS)
        mixed = dot(hidden[step % 2], w2[...])
        normed = layer_norm(mixed, gain[layer : layer + 1, :], shift[layer : layer + 1, :])
        fresh_held[rows, :] = (edge_in[rows, :].astype(jnp.float32) + normed).astype(NARROW)

    for step in range(steps + 1):
        if step < steps:
            head(step)
        if step > 0:
            tail(step - 1)
            if last:
                part = pl.ds((step - 1) * ROWS, ROWS)
                target = edge_out.at[part, :]
                carried.append(fetch(fresh_held.at[part, :], target, refs[1].at[step - 1]))
    total = dot(flip_in[...], fresh_held[...])
    near = {k - plan.reach: plan.block(total, k) for k in range(plan.span)}
    far = total[plan.near_total :, :]
    kept_out[...] = jnp.concatenate([near[0], far[: plan.column_rows, :]], axis=0).astype(NARROW)
    plan.column_outs(column_outs, near, far)
    for copy in carried:
        copy.wait()


def node_kernel(plan, layer, last, nodes, near_table, far_table, near_in, *refs):
    line_ins, refs = refs[: plan.lines - 1], refs[plan.lines - 1 :]
    w1, b1, w2, gain, shift, node_out, *outs = refs
    states = nodes[...]
    rows, features = states.shape
    _, f = plan.here()
    summed = jnp.zeros(states.shape, jnp.float32)
    for k in range(plan.span):
        offset = k - plan.reach
        part = plan.block(near_in, k)
        if offset:
            part = jnp.where(
                plan.leaves(f, offset), plan.block(line_ins[0], abs(offset) - 1), part
            )
        summed += dot(hot(iota((rows, plan.near), 0), near_table[k]), part.astype(NARROW))
    far = [plan.tail(ref, plan.line_rows) for ref in (near_in, *line_ins)]
    picks = hot(iota((plan.far_total, rows), 1), far_rows(plan, far_table))
    summed += dot_rows(picks, jnp.concatenate(far, axis=0).astype(NARROW))
    pre = dot(states, w1[:features, :])
    pre += dot(summed.astype(NARROW), w1[features:, :])
    hidden = silu(pre + b1[layer : layer + 1, :]).astype(NARROW)
    mixed = dot(hidden, w2[...])
    normed = layer_norm(mixed, gain[layer : layer + 1, :], shift[layer : layer + 1, :])
    fresh = (states.astype(jnp.float32) + normed).astype(NARROW)
    node_out[...] = fresh
    if not last:
        place(plan, fresh, near_table, picks, outs[0], outs[1:])


def cost(flops, moved):
    return pl.CostEstimate(flops=flops, bytes_accessed=moved, transcendentals=0)


def stay(array):
    return pltpu.with_memory_space_constraint(array, pltpu.HBM)


def near_by(shape):
    return pltpu.VMEM(shape, NARROW)


LOCAL = pl.BlockSpec(memory_space=pltpu.VMEM)
AWAY = pl.BlockSpec(memory_space=pl.ANY)


def call(kernel, name, limit, inputs, outputs, work, scratch=()):
    return pl.pallas_call(
        kernel,
        out_shape=[shape for _, shape in outputs],
        in_specs=[spec for spec, _ in inputs],
        out_specs=[spec for spec, _ in outputs],
        scratch_shapes=list(scratch),
        compiler_params=pltpu.CompilerParams(vmem_limit_bytes=limit << 20),
        cost_estimate=work,
        name=name,
    )(*[array for _, array in inputs])


def on_device(
    nodes,
    edges,
    near_table,
    far_table,
    edge_sender,
    edge_receiver,
    edge_w1,
    edge_b1,
    edge_w2,
    edge_gain,
    edge_shift,
    node_w1,
    node_b1,
    node_w2,
    node_gain,
    node_shift,
):
    near_table = near_table.transpose(1, 0, 2)
    far_table = far_table.transpose(0, 2, 1)
    plan = Plan(near_table.shape, far_table.shape)
    node_rows, features = nodes.shape
    edge_rows = edges.shape[0]
    layers = edge_w1.shape[0]
    hot_width = -(-2 * plan.slots // LANES) * LANES
    wide = (edge_rows, features)
    lines, columns = range(1, plan.lines), range(1, plan.columns)
    own_shape = near_by((plan.near_total + plan.line_rows, features))
    kept_shape = near_by((plan.near + plan.column_rows, features))
    far_shape = near_by((plan.column_rows, features))
    line_shapes = [near_by((plan.line_message(a), features)) for a in lines]
    column_shapes = [near_by((plan.column_message(e), features)) for e in columns]
    weight_shapes = [near_by((2 * features, features)), near_by((features, features))]

    def local(arrays):
        return [(LOCAL, array) for array in arrays]

    def away(arrays):
        return [(AWAY, stay(array)) for array in arrays]

    small = cost(4 * plan.slots * node_rows * features, 4 * plan.slots * features)
    tables = [near_table, far_table]
    own, *lines_out = call(
        functools.partial(place_kernel, plan),
        "place",
        8,
        local([nodes, *tables]),
        local([own_shape, *line_shapes]),
        small,
    )
    sender = edge_sender.reshape(edge_rows // LANES, LANES)
    receiver = edge_receiver.reshape(edge_rows // LANES, LANES)
    hot_rows, flip, start, edge_state, *weights = call(
        functools.partial(prep_kernel, plan, 0),
        "prep",
        8,
        local([sender, receiver]) + away([edges, edge_w1, edge_w2]) + local([edge_b1]),
        local(
            [
                near_by((edge_rows, hot_width)),
                near_by((plan.slots, edge_rows)),
                near_by(wide),
                near_by(wide),
                *weight_shapes,
            ]
        ),
        cost(2 * edge_rows * features * features, 8 * edge_rows * features),
        [
            pltpu.VMEM((features, features), NARROW),
            pltpu.SemaphoreType.DMA((edge_rows // ROWS,)),
            pltpu.SemaphoreType.DMA((3,)),
        ],
    )
    states = nodes
    for layer in range(layers):
        last = layer == layers - 1
        lines_in = [along_node(block, a) for a, block in zip(lines, lines_out)]
        if layer > 0:
            start, *weights = call(
                functools.partial(start_kernel, layer),
                "start",
                8,
                local([edge_state]) + away([edge_w1, edge_w2]) + local([edge_b1]),
                local([near_by(wide), *weight_shapes]),
                cost(2 * edge_rows * features * features, 4 * edge_rows * features),
                [
                    pltpu.VMEM((features, features), NARROW),
                    pltpu.SemaphoreType.DMA((3,)),
                ],
            )
        far_first, *columns_out = call(
            functools.partial(turn_out_kernel, plan),
            "turn_out",
            8,
            local([own, *lines_in]),
            local([far_shape, *column_shapes]),
            small,
        )
        columns_in = [along_feat(block, e) for e, block in zip(columns, columns_out)]
        scratch = [
            pltpu.VMEM((2, ROWS, features), NARROW),
            pltpu.VMEM((hot_width, features), NARROW),
            pltpu.SemaphoreType.DMA((2,)),
        ]
        if last:
            scratch.append(pltpu.VMEM(wide, NARROW))
            scratch.append(pltpu.SemaphoreType.DMA((edge_rows // ROWS,)))
        edge_shape = (AWAY, pltpu.HBM(wide, NARROW)) if last else (LOCAL, near_by(wide))
        edge_state, kept, *rest = call(
            functools.partial(edge_kernel, plan, layer, last),
            "edge",
            16,
            local([hot_rows, flip, start, edge_state, *weights, edge_gain, edge_shift])
            + local([own, far_first, *columns_in])
            + away([node_w1, node_w2]),
            [edge_shape] + local([kept_shape, *column_shapes, *weight_shapes]),
            cost(
                2 * edge_rows * features * (hot_width + features + plan.slots),
                10 * edge_rows * features,
            ),
            scratch,
        )
        columns_back, (node_first, node_second) = rest[:-2], rest[-2:]
        columns_in = [along_feat(block, -e) for e, block in zip(columns, columns_back)]
        near_sums, *lines_back = call(
            functools.partial(turn_back_kernel, plan),
            "turn_back",
            8,
            local([kept, *columns_in]),
            local([own_shape, *line_shapes]),
            small,
        )
        lines_in = [along_node(block, -a) for a, block in zip(lines, lines_back)]
        out_shape = [jax.ShapeDtypeStruct(nodes.shape, NARROW)] if last else [near_by(nodes.shape)]
        outs = call(
            functools.partial(node_kernel, plan, layer, last),
            "node",
            8,
            local([states, *tables, near_sums, *lines_in])
            + local([node_first, node_b1, node_second, node_gain, node_shift]),
            local(out_shape + ([] if last else [own_shape, *line_shapes])),
            small,
        )
        states = outs[0]
        if not last:
            own, *lines_out = outs[1:]
    return (states, edge_state)


def solution(mesh):
    split = ("ens", "node", "feat")
    return jax.shard_map(
        on_device,
        mesh=mesh,
        in_specs=(
            P(split, None),
            P(split, None),
            P(split, None, None),
            P(split, None, None),
            P(split),
            P(split),
        )
        + (P(),) * 10,
        out_specs=(P(split, None), P(split, None)),
        check_vma=False,
    )
```

```python
import functools

import jax
import jax.numpy as jnp
from jax import lax
from jax.experimental import pallas as pl
from jax.experimental.pallas import tpu as pltpu
from jax.sharding import PartitionSpec as P

EPSILON = 1e-05
PEERS = ("node", "feat")
ROWS = 256
LANES = 128
NARROW = jnp.bfloat16


def grid_size():
    return lax.axis_size("node"), lax.axis_size("feat")


def side(column, columns):
    return 1 if column >= columns // 2 else -1


def along_node(block, distance):
    lines, columns = grid_size()
    route = []
    for z in range(lines):
        for f in range(columns):
            target = (z + side(f, columns) * distance) % lines
            route.append((z * columns + f, target * columns + f))
    return lax.ppermute(block, PEERS, route)


def along_feat(block, distance):
    lines, columns = grid_size()
    route = []
    for z in range(lines):
        for f in range(columns):
            route.append((z * columns + f, z * columns + (f + distance) % columns))
    return lax.ppermute(block, PEERS, route)


def dot(left, right):
    return jnp.dot(left, right, preferred_element_type=jnp.float32)


def dot_rows(left, right):
    return lax.dot_general(
        left, right, (((0,), (0,)), ((), ())), preferred_element_type=jnp.float32
    )


def silu(values):
    half = 0.5 * values
    return half * jnp.tanh(half) + half


def layer_norm(values, norm_gain, norm_shift):
    center = values - jnp.mean(values, axis=-1, keepdims=True)
    spread = jnp.mean(center * center, axis=-1, keepdims=True)
    return center * lax.rsqrt(spread + EPSILON) * norm_gain + norm_shift


def iota(shape, axis):
    return lax.broadcasted_iota(jnp.int32, shape, axis)


def hot(left, right):
    return jnp.where(left == right, 1.0, 0.0).astype(NARROW)


class Plan:
    def __init__(self, near_shape, far_shape):
        self.lines, self.columns = grid_size()
        self.span, _, self.near = near_shape
        self.reach = (self.span - 1) // 2
        self.width = far_shape[1]
        self.line_rows = self.columns * self.width
        self.column_rows = self.lines * self.width
        self.near_total = self.span * self.near
        self.far_total = self.lines * self.line_rows
        self.slots = self.near_total + self.far_total
        self.offsets = [o for o in range(-self.reach, self.reach + 1) if o]

    def here(self):
        return lax.axis_index("node"), lax.axis_index("feat")

    def upper(self, column):
        return column >= self.columns // 2

    def leaves(self, column, offset):
        return jnp.logical_or(column + offset < 0, column + offset >= self.columns)

    def near_in(self, e):
        return [o for o in self.offsets if o % self.columns == e]

    def line_message(self, a):
        return (self.reach * self.near if a == 1 else 0) + self.line_rows

    def column_message(self, e):
        return len(self.near_in(e)) * self.near + self.column_rows

    def block(self, ref, index):
        return ref[index * self.near : (index + 1) * self.near, :].astype(jnp.float32)

    def tail(self, ref, count):
        rows = ref.shape[0]
        return ref[rows - count : rows, :].astype(jnp.float32)

    def line_outs(self, outs, near, far, column):
        for a, out in enumerate(outs, 1):
            parts = [far[a * self.line_rows : (a + 1) * self.line_rows, :]]
            if a == 1:
                upper = self.upper(column)
                relayed = [
                    jnp.where(upper, near[i], near[-i]) for i in range(1, self.reach + 1)
                ]
                parts = relayed + parts
            out[...] = jnp.concatenate(parts, axis=0).astype(out.dtype)

    def column_outs(self, outs, near, far):
        for e, out in enumerate(outs, 1):
            parts = [near[o] for o in self.near_in(e)]
            parts.append(far[e * self.column_rows : (e + 1) * self.column_rows, :])
            out[...] = jnp.concatenate(parts, axis=0).astype(out.dtype)

    def column_near(self, ins):
        near = {}
        for e, ref in enumerate(ins, 1):
            for i, o in enumerate(self.near_in(e)):
                near[o] = self.block(ref, i)
        return near

    def reorder(self, far, outer):
        total = self.far_total
        inner = total // (outer * self.width)
        row = iota((total, total), 0)
        c, rest = row % self.width, row // self.width
        source = ((rest % outer) * inner + rest // outer) * self.width + c
        return dot(hot(iota((total, total), 1), source), far.astype(NARROW))


def far_rows(plan, far_ref):
    z, f = plan.here()
    table = far_ref[0].astype(jnp.float32)
    width, peers = table.shape
    total = peers * width
    row = iota((total, peers), 0)
    e = (row // width) % plan.columns
    a = row // plan.line_rows
    a = jnp.where(plan.upper(f), a, plan.lines - a)
    peer = ((z + a) % plan.lines) * plan.columns + (f + e) % plan.columns
    spread = jnp.where(peer == iota((total, peers), 1), 1.0, 0.0)
    wide = lax.dot_general(
        spread,
        table,
        (((1,), (1,)), ((), ())),
        preferred_element_type=jnp.float32,
        precision=lax.Precision.HIGHEST,
    )
    own = iota((total, width), 0) % width == iota((total, width), 1)
    return jnp.sum(jnp.where(own, wide, 0.0), axis=1, keepdims=True).astype(jnp.int32)


def place(plan, states, near_ref, picks_far, own_out, line_outs):
    rows = states.shape[0]
    near = {}
    for k in range(plan.span):
        picks = hot(iota((rows, plan.near), 0), near_ref[k])
        near[k - plan.reach] = dot_rows(picks, states)
    far = dot(picks_far, states)
    own = [near[k - plan.reach] for k in range(plan.span)] + [far[: plan.line_rows, :]]
    own_out[...] = jnp.concatenate(own, axis=0).astype(own_out.dtype)
    plan.line_outs(line_outs, near, far, plan.here()[1])


def place_kernel(plan, nodes, near, far, own_out, *refs):
    line_outs, held = refs[: plan.lines - 1], refs[plan.lines - 1 : -1]
    copies = [fetch(a, b, refs[-1].at[i]) for i, (a, b) in enumerate(zip((far, near, nodes), held))]
    far_held, near_held, states = held
    copies[0].wait()
    picks = hot(iota((plan.far_total, states.shape[0]), 1), far_rows(plan, far_held))
    for copy in copies[1:]:
        copy.wait()
    place(plan, states[...], near_held, picks, own_out, line_outs)


def turn_out_kernel(plan, own, _, *refs):
    line_ins, far_out = refs[: plan.lines - 1], refs[plan.lines - 1]
    column_outs = refs[plan.lines :]
    _, f = plan.here()
    near = {}
    for o in plan.offsets:
        mine = plan.block(own, o + plan.reach)
        near[o] = jnp.where(plan.leaves(f, o), plan.block(line_ins[0], abs(o) - 1), mine)
    far = [plan.tail(ref, plan.line_rows) for ref in (own, *line_ins)]
    far = plan.reorder(jnp.concatenate(far, axis=0), plan.lines)
    far_out[...] = far[: plan.column_rows, :].astype(far_out.dtype)
    plan.column_outs(column_outs, near, far)


def turn_back_kernel(plan, kept, *refs):
    column_ins, near_out = refs[: plan.columns - 1], refs[plan.columns - 1]
    line_outs = refs[plan.columns :]
    _, f = plan.here()
    near = plan.column_near(column_ins)
    near[0] = plan.block(kept, 0)
    far = [plan.tail(ref, plan.column_rows) for ref in (kept, *column_ins)]
    far = plan.reorder(jnp.concatenate(far, axis=0), plan.columns)
    own = [near[k - plan.reach] for k in range(plan.span)] + [far[: plan.line_rows, :]]
    near_out[...] = jnp.concatenate(own, axis=0).astype(near_out.dtype)
    plan.line_outs(line_outs, near, far, f)


def fetch(source, target, sem):
    copy = pltpu.make_async_copy(source, target, sem)
    copy.start()
    return copy


def in_order(plan, slot):
    z, f = plan.here()
    t = jnp.maximum(slot - plan.near_total, 0)
    c, p = t % plan.width, t // plan.width
    line, column = p // plan.columns, p % plan.columns
    e = (f - column + plan.columns) % plan.columns
    away = jnp.where(plan.upper(column), z - line, line - z)
    a = (away + plan.lines) % plan.lines
    renamed = plan.near_total + (e * plan.lines + a) * plan.width + c
    return jnp.where(slot < plan.near_total, slot, renamed)


def hots_kernel(plan, sender, receiver, edges, hot_out, flip_out, edge_out, *refs):
    sender_held, receiver_held, sems = refs
    slots = plan.slots
    edge_rows, width = hot_out.shape
    copies = [
        fetch(sender, sender_held, sems.at[0]),
        fetch(receiver, receiver_held, sems.at[1]),
        fetch(edges, edge_out, sems.at[2]),
    ]
    copies[0].wait()
    copies[1].wait()
    sent = in_order(plan, sender_held[...])
    received = in_order(plan, receiver_held[...])
    for index in range(edge_rows // LANES):
        rows = slice(index * LANES, (index + 1) * LANES)
        hot_s = jnp.where(iota((slots, LANES), 0) == sent[index : index + 1, :], 1.0, 0.0)
        hot_r = jnp.where(iota((slots, LANES), 0) == received[index : index + 1, :], 1.0, 0.0)
        flip_out[:, rows] = hot_r.astype(NARROW)
        pad = jnp.zeros((width - 2 * slots, LANES), jnp.float32)
        both = jnp.concatenate([hot_s, hot_r, pad], axis=0)
        hot_out[rows, :] = both.T.astype(NARROW)
    copies[2].wait()


def start_kernel(layer, edges, w1, w2, b1, _, start_out, w1_out, w2_out, weight, bias, w_sems):
    features = weight.shape[0]
    zeroth = fetch(b1, bias, w_sems.at[3])
    first = fetch(w1.at[layer, pl.ds(0, features), :], weight, w_sems.at[0])
    second = fetch(w1.at[layer, pl.ds(features, 2 * features), :], w1_out, w_sems.at[1])
    third = fetch(w2.at[layer], w2_out, w_sems.at[2])
    zeroth.wait()
    first.wait()
    for step in range(edges.shape[0] // ROWS):
        rows = slice(step * ROWS, (step + 1) * ROWS)
        start = dot(edges[rows, :], weight[...]) + bias[layer : layer + 1, :]
        start_out[rows, :] = start.astype(start_out.dtype)
    second.wait()
    third.wait()


def edge_kernel(plan, layer, last, hot_in, flip_in, start_in, edge_in, w1, w2, gain, shift, *refs):
    own, far_first, *refs = refs
    column_ins, refs = refs[: plan.columns - 1], refs[plan.columns - 1 :]
    node_w1, node_w2, edge_out, kept_out, *refs = refs
    column_outs, refs = refs[: plan.columns - 1], refs[plan.columns - 1 :]
    w1_out, w2_out, hidden, table, w_sems, *refs = refs
    steps = edge_in.shape[0] // ROWS
    slots, features = plan.slots, edge_in.shape[1]
    carried = [
        fetch(node_w1.at[layer], w1_out, w_sems.at[0]),
        fetch(node_w2.at[layer], w2_out, w_sems.at[1]),
    ]
    near = plan.column_near(column_ins)
    near[0] = plan.block(own, plan.reach)
    arrived = [near[k - plan.reach] for k in range(plan.span)]
    arrived += [plan.tail(ref, plan.column_rows) for ref in (far_first, *column_ins)]
    arrived = jnp.concatenate(arrived, axis=0).astype(NARROW)
    rest = table.shape[0] - 2 * slots
    table[2 * slots :, :] = jnp.zeros((rest, features), NARROW)
    table[0:slots, :] = dot(arrived, w1[:features, :]).astype(NARROW)
    table[slots : 2 * slots, :] = dot(arrived, w1[features:, :]).astype(NARROW)
    fresh_held = refs[0] if last else edge_out

    def head(step):
        rows = slice(step * ROWS, (step + 1) * ROWS)
        pre = dot(hot_in[rows, :], table[...]) + start_in[rows, :].astype(jnp.float32)
        hidden[step % 2] = silu(pre).astype(NARROW)

    def tail(step):
        rows = slice(step * ROWS, (step + 1) * ROWS)
        mixed = dot(hidden[step % 2], w2[...])
        normed = layer_norm(mixed, gain[layer : layer + 1, :], shift[layer : layer + 1, :])
        fresh_held[rows, :] = (edge_in[rows, :].astype(jnp.float32) + normed).astype(NARROW)

    for step in range(steps + 1):
        if step < steps:
            head(step)
        if step > 0:
            tail(step - 1)
            if last:
                part = pl.ds((step - 1) * ROWS, ROWS)
                target = edge_out.at[part, :]
                carried.append(fetch(fresh_held.at[part, :], target, refs[1].at[step - 1]))
    total = dot(flip_in[...], fresh_held[...])
    near = {k - plan.reach: plan.block(total, k) for k in range(plan.span)}
    far = total[plan.near_total :, :]
    kept_out[...] = jnp.concatenate([near[0], far[: plan.column_rows, :]], axis=0).astype(NARROW)
    plan.column_outs(column_outs, near, far)
    for copy in carried:
        copy.wait()


def node_kernel(plan, layer, last, nodes, near_table, far_table, near_in, *refs):
    line_ins, refs = refs[: plan.lines - 1], refs[plan.lines - 1 :]
    w1, b1, w2, gain, shift, node_out, *outs = refs
    states = nodes[...]
    rows, features = states.shape
    _, f = plan.here()
    summed = jnp.zeros(states.shape, jnp.float32)
    for k in range(plan.span):
        offset = k - plan.reach
        part = plan.block(near_in, k)
        if offset:
            part = jnp.where(
                plan.leaves(f, offset), plan.block(line_ins[0], abs(offset) - 1), part
            )
        summed += dot(hot(iota((rows, plan.near), 0), near_table[k]), part.astype(NARROW))
    far = [plan.tail(ref, plan.line_rows) for ref in (near_in, *line_ins)]
    picks = hot(iota((plan.far_total, rows), 1), far_rows(plan, far_table))
    summed += dot_rows(picks, jnp.concatenate(far, axis=0).astype(NARROW))
    pre = dot(states, w1[:features, :])
    pre += dot(summed.astype(NARROW), w1[features:, :])
    hidden = silu(pre + b1[layer : layer + 1, :]).astype(NARROW)
    mixed = dot(hidden, w2[...])
    normed = layer_norm(mixed, gain[layer : layer + 1, :], shift[layer : layer + 1, :])
    fresh = (states.astype(jnp.float32) + normed).astype(NARROW)
    node_out[...] = fresh
    if not last:
        place(plan, fresh, near_table, picks, outs[0], outs[1:])


def cost(flops, moved):
    return pl.CostEstimate(flops=flops, bytes_accessed=moved, transcendentals=0)


def stay(array):
    return pltpu.with_memory_space_constraint(array, pltpu.HBM)


def near_by(shape):
    return pltpu.VMEM(shape, NARROW)


LOCAL = pl.BlockSpec(memory_space=pltpu.VMEM)
AWAY = pl.BlockSpec(memory_space=pl.ANY)


def call(kernel, name, limit, inputs, outputs, work, scratch=()):
    return pl.pallas_call(
        kernel,
        out_shape=[shape for _, shape in outputs],
        in_specs=[spec for spec, _ in inputs],
        out_specs=[spec for spec, _ in outputs],
        scratch_shapes=list(scratch),
        compiler_params=pltpu.CompilerParams(vmem_limit_bytes=limit << 20),
        cost_estimate=work,
        name=name,
    )(*[array for _, array in inputs])


def on_device(
    nodes,
    edges,
    near_table,
    far_table,
    edge_sender,
    edge_receiver,
    edge_w1,
    edge_b1,
    edge_w2,
    edge_gain,
    edge_shift,
    node_w1,
    node_b1,
    node_w2,
    node_gain,
    node_shift,
):
    near_table = near_table.transpose(1, 0, 2)
    far_table = far_table.transpose(0, 2, 1)
    plan = Plan(near_table.shape, far_table.shape)
    node_rows, features = nodes.shape
    edge_rows = edges.shape[0]
    layers = edge_w1.shape[0]
    hot_width = -(-2 * plan.slots // LANES) * LANES
    wide = (edge_rows, features)
    lines, columns = range(1, plan.lines), range(1, plan.columns)
    own_shape = near_by((plan.near_total + plan.line_rows, features))
    kept_shape = near_by((plan.near + plan.column_rows, features))
    far_shape = near_by((plan.column_rows, features))
    line_shapes = [near_by((plan.line_message(a), features)) for a in lines]
    column_shapes = [near_by((plan.column_message(e), features)) for e in columns]
    weight_shapes = [near_by((2 * features, features)), near_by((features, features))]

    def local(arrays):
        return [(LOCAL, array) for array in arrays]

    def away(arrays):
        return [(AWAY, stay(array)) for array in arrays]

    small = cost(4 * plan.slots * node_rows * features, 4 * plan.slots * features)
    tables = [near_table, far_table]
    own, *lines_out = call(
        functools.partial(place_kernel, plan),
        "place",
        8,
        away([nodes, *tables]),
        local([own_shape, *line_shapes]),
        small,
        [
            pltpu.VMEM(far_table.shape, jnp.int32),
            pltpu.VMEM(near_table.shape, jnp.int32),
            pltpu.VMEM(nodes.shape, NARROW),
            pltpu.SemaphoreType.DMA((3,)),
        ],
    )
    index_shape = (edge_rows // LANES, LANES)
    hot_rows, flip, edge_state = call(
        functools.partial(hots_kernel, plan),
        "hots",
        8,
        away([edge_sender.reshape(index_shape), edge_receiver.reshape(index_shape), edges]),
        local([near_by((edge_rows, hot_width)), near_by((plan.slots, edge_rows)), near_by(wide)]),
        cost(2 * edge_rows * features * features, 8 * edge_rows * features),
        [
            pltpu.VMEM(index_shape, jnp.int32),
            pltpu.VMEM(index_shape, jnp.int32),
            pltpu.SemaphoreType.DMA((3,)),
        ],
    )
    states = nodes
    for layer in range(layers):
        last = layer == layers - 1
        lines_in = [along_node(block, a) for a, block in zip(lines, lines_out)]
        far_first, *columns_out = call(
            functools.partial(turn_out_kernel, plan),
            "turn_out",
            8,
            local([own, flip, *lines_in]),
            local([far_shape, *column_shapes]),
            small,
        )
        start, *weights = call(
            functools.partial(start_kernel, layer),
            "start",
            8,
            local([edge_state])
            + away([edge_w1, edge_w2, edge_b1])
            + local([far_first if layer == 0 else own]),
            local([near_by(wide), *weight_shapes]),
            cost(2 * edge_rows * features * features, 4 * edge_rows * features),
            [
                pltpu.VMEM((features, features), NARROW),
                pltpu.VMEM(edge_b1.shape, jnp.float32),
                pltpu.SemaphoreType.DMA((4,)),
            ],
        )
        columns_in = [along_feat(block, e) for e, block in zip(columns, columns_out)]
        scratch = [
            pltpu.VMEM((2, ROWS, features), NARROW),
            pltpu.VMEM((hot_width, features), NARROW),
            pltpu.SemaphoreType.DMA((2,)),
        ]
        if last:
            scratch.append(pltpu.VMEM(wide, NARROW))
            scratch.append(pltpu.SemaphoreType.DMA((edge_rows // ROWS,)))
        edge_shape = (AWAY, pltpu.HBM(wide, NARROW)) if last else (LOCAL, near_by(wide))
        edge_state, kept, *rest = call(
            functools.partial(edge_kernel, plan, layer, last),
            "edge",
            16,
            local([hot_rows, flip, start, edge_state, *weights, edge_gain, edge_shift])
            + local([own, far_first, *columns_in])
            + away([node_w1, node_w2]),
            [edge_shape] + local([kept_shape, *column_shapes, *weight_shapes]),
            cost(
                2 * edge_rows * features * (hot_width + features + plan.slots),
                10 * edge_rows * features,
            ),
            scratch,
        )
        columns_back, (node_first, node_second) = rest[:-2], rest[-2:]
        columns_in = [along_feat(block, -e) for e, block in zip(columns, columns_back)]
        near_sums, *lines_back = call(
            functools.partial(turn_back_kernel, plan),
            "turn_back",
            8,
            local([kept, *columns_in]),
            local([own_shape, *line_shapes]),
            small,
        )
        lines_in = [along_node(block, -a) for a, block in zip(lines, lines_back)]
        out_shape = [jax.ShapeDtypeStruct(nodes.shape, NARROW)] if last else [near_by(nodes.shape)]
        outs = call(
            functools.partial(node_kernel, plan, layer, last),
            "node",
            8,
            local([states, *tables, near_sums, *lines_in])
            + local([node_first, node_b1, node_second, node_gain, node_shift]),
            local(out_shape + ([] if last else [own_shape, *line_shapes])),
            small,
        )
        states = outs[0]
        if not last:
            own, *lines_out = outs[1:]
    return (states, edge_state)


def solution(mesh):
    split = ("ens", "node", "feat")
    return jax.shard_map(
        on_device,
        mesh=mesh,
        in_specs=(
            P(split, None),
            P(split, None),
            P(split, None, None),
            P(split, None, None),
            P(split),
            P(split),
        )
        + (P(),) * 10,
        out_specs=(P(split, None), P(split, None)),
        check_vma=False,
    )
```

```python
import functools

import jax
import jax.numpy as jnp
from jax import lax
from jax.experimental import pallas as pl
from jax.experimental.pallas import tpu as pltpu
from jax.sharding import PartitionSpec as P

EPSILON = 1e-05
PEERS = ("node", "feat")
ROWS = 256
EDGE_ROWS = 512
LANES = 128
NARROW = jnp.bfloat16


def grid_size():
    return lax.axis_size("node"), lax.axis_size("feat")


def side(column, columns):
    return 1 if column >= columns // 2 else -1


def along_node(block, distance):
    lines, columns = grid_size()
    route = []
    for z in range(lines):
        for f in range(columns):
            target = (z + side(f, columns) * distance) % lines
            route.append((z * columns + f, target * columns + f))
    return lax.ppermute(block, PEERS, route)


def along_feat(block, distance):
    lines, columns = grid_size()
    route = []
    for z in range(lines):
        for f in range(columns):
            route.append((z * columns + f, z * columns + (f + distance) % columns))
    return lax.ppermute(block, PEERS, route)


def dot(left, right):
    return jnp.dot(left, right, preferred_element_type=jnp.float32)


def dot_rows(left, right):
    return lax.dot_general(
        left, right, (((0,), (0,)), ((), ())), preferred_element_type=jnp.float32
    )


def silu_of_half(half):
    return half * jnp.tanh(half) + half


def silu(values):
    return silu_of_half(0.5 * values)


def layer_norm(values, norm_gain, norm_shift):
    center = values - jnp.mean(values, axis=-1, keepdims=True)
    return scaled(center, norm_gain, norm_shift)


def scaled(center, norm_gain, norm_shift):
    spread = jnp.mean(center * center, axis=-1, keepdims=True)
    return center * lax.rsqrt(spread + EPSILON) * norm_gain + norm_shift


def iota(shape, axis):
    return lax.broadcasted_iota(jnp.int32, shape, axis)


def hot(left, right):
    return jnp.where(left == right, 1.0, 0.0).astype(NARROW)


class Plan:
    def __init__(self, near_shape, far_shape):
        self.lines, self.columns = grid_size()
        self.span, _, self.near = near_shape
        self.reach = (self.span - 1) // 2
        self.width = far_shape[1]
        self.line_rows = self.columns * self.width
        self.column_rows = self.lines * self.width
        self.near_total = self.span * self.near
        self.far_total = self.lines * self.line_rows
        self.slots = self.near_total + self.far_total
        self.offsets = [o for o in range(-self.reach, self.reach + 1) if o]

    def here(self):
        return lax.axis_index("node"), lax.axis_index("feat")

    def upper(self, column):
        return column >= self.columns // 2

    def leaves(self, column, offset):
        return jnp.logical_or(column + offset < 0, column + offset >= self.columns)

    def near_in(self, e):
        return [o for o in self.offsets if o % self.columns == e]

    def line_message(self, a):
        return (self.reach * self.near if a == 1 else 0) + self.line_rows

    def column_message(self, e):
        return len(self.near_in(e)) * self.near + self.column_rows

    def block(self, ref, index):
        return ref[index * self.near : (index + 1) * self.near, :].astype(jnp.float32)

    def tail(self, ref, count):
        rows = ref.shape[0]
        return ref[rows - count : rows, :].astype(jnp.float32)

    def line_outs(self, outs, near, far, column):
        for a, out in enumerate(outs, 1):
            parts = [far[a * self.line_rows : (a + 1) * self.line_rows, :]]
            if a == 1:
                upper = self.upper(column)
                relayed = [
                    jnp.where(upper, near[i], near[-i]) for i in range(1, self.reach + 1)
                ]
                parts = relayed + parts
            out[...] = jnp.concatenate(parts, axis=0).astype(out.dtype)

    def column_outs(self, outs, near, far):
        for e, out in enumerate(outs, 1):
            parts = [near[o] for o in self.near_in(e)]
            parts.append(far[e * self.column_rows : (e + 1) * self.column_rows, :])
            out[...] = jnp.concatenate(parts, axis=0).astype(out.dtype)

    def column_near(self, ins):
        near = {}
        for e, ref in enumerate(ins, 1):
            for i, o in enumerate(self.near_in(e)):
                near[o] = self.block(ref, i)
        return near

    def reorder(self, far, outer):
        total = self.far_total
        inner = total // (outer * self.width)
        row = iota((total, total), 0)
        c, rest = row % self.width, row // self.width
        source = ((rest % outer) * inner + rest // outer) * self.width + c
        return dot(hot(iota((total, total), 1), source), far.astype(NARROW))


def far_rows(plan, far_ref):
    z, f = plan.here()
    table = far_ref[0].astype(jnp.float32)
    width, peers = table.shape
    total = peers * width
    row = iota((total, peers), 0)
    e = (row // width) % plan.columns
    a = row // plan.line_rows
    a = jnp.where(plan.upper(f), a, plan.lines - a)
    peer = ((z + a) % plan.lines) * plan.columns + (f + e) % plan.columns
    spread = jnp.where(peer == iota((total, peers), 1), 1.0, 0.0)
    wide = lax.dot_general(
        spread,
        table,
        (((1,), (1,)), ((), ())),
        preferred_element_type=jnp.float32,
        precision=lax.Precision.HIGHEST,
    )
    own = iota((total, width), 0) % width == iota((total, width), 1)
    return jnp.sum(jnp.where(own, wide, 0.0), axis=1, keepdims=True).astype(jnp.int32)


def place(plan, states, near_ref, picks_far, own_out, line_outs):
    rows = states.shape[0]
    near = {}
    for k in range(plan.span):
        picks = hot(iota((rows, plan.near), 0), near_ref[k])
        near[k - plan.reach] = dot_rows(picks, states)
    far = dot(picks_far, states)
    own = [near[k - plan.reach] for k in range(plan.span)] + [far[: plan.line_rows, :]]
    own_out[...] = jnp.concatenate(own, axis=0).astype(own_out.dtype)
    plan.line_outs(line_outs, near, far, plan.here()[1])


def place_kernel(plan, nodes, near, far, own_out, *refs):
    line_outs, held = refs[: plan.lines - 1], refs[plan.lines - 1 : -1]
    copies = [fetch(a, b, refs[-1].at[i]) for i, (a, b) in enumerate(zip((far, near, nodes), held))]
    far_held, near_held, states = held
    copies[0].wait()
    picks = hot(iota((plan.far_total, states.shape[0]), 1), far_rows(plan, far_held))
    for copy in copies[1:]:
        copy.wait()
    place(plan, states[...], near_held, picks, own_out, line_outs)


def turn_out_kernel(plan, own, _, *refs):
    line_ins, far_out = refs[: plan.lines - 1], refs[plan.lines - 1]
    column_outs = refs[plan.lines :]
    _, f = plan.here()
    near = {}
    for o in plan.offsets:
        mine = plan.block(own, o + plan.reach)
        near[o] = jnp.where(plan.leaves(f, o), plan.block(line_ins[0], abs(o) - 1), mine)
    far = [plan.tail(ref, plan.line_rows) for ref in (own, *line_ins)]
    far = plan.reorder(jnp.concatenate(far, axis=0), plan.lines)
    far_out[...] = far[: plan.column_rows, :].astype(far_out.dtype)
    plan.column_outs(column_outs, near, far)


def turn_back_kernel(plan, kept, *refs):
    column_ins, near_out = refs[: plan.columns - 1], refs[plan.columns - 1]
    line_outs = refs[plan.columns :]
    _, f = plan.here()
    near = plan.column_near(column_ins)
    near[0] = plan.block(kept, 0)
    far = [plan.tail(ref, plan.column_rows) for ref in (kept, *column_ins)]
    far = plan.reorder(jnp.concatenate(far, axis=0), plan.columns)
    own = [near[k - plan.reach] for k in range(plan.span)] + [far[: plan.line_rows, :]]
    near_out[...] = jnp.concatenate(own, axis=0).astype(near_out.dtype)
    plan.line_outs(line_outs, near, far, f)


def fetch(source, target, sem):
    copy = pltpu.make_async_copy(source, target, sem)
    copy.start()
    return copy


def in_order(plan, slot):
    z, f = plan.here()
    t = jnp.maximum(slot - plan.near_total, 0)
    c, p = t % plan.width, t // plan.width
    line, column = p // plan.columns, p % plan.columns
    e = (f - column + plan.columns) % plan.columns
    away = jnp.where(plan.upper(column), z - line, line - z)
    a = (away + plan.lines) % plan.lines
    renamed = plan.near_total + (e * plan.lines + a) * plan.width + c
    return jnp.where(slot < plan.near_total, slot, renamed)


def hots_kernel(plan, sender, receiver, edges, w1, w2, hot_out, flip_out, edge_out, *refs):
    w1_out, w2_out, sender_held, receiver_held, sems = refs
    slots = plan.slots
    edge_rows, width = hot_out.shape
    copies = [
        fetch(sender, sender_held, sems.at[0]),
        fetch(receiver, receiver_held, sems.at[1]),
        fetch(edges, edge_out, sems.at[2]),
        fetch(w1, w1_out, sems.at[3]),
        fetch(w2, w2_out, sems.at[4]),
    ]
    copies[0].wait()
    copies[1].wait()
    sent = in_order(plan, sender_held[...])
    received = in_order(plan, receiver_held[...])
    for index in range(edge_rows // LANES):
        rows = slice(index * LANES, (index + 1) * LANES)
        hot_s = jnp.where(iota((slots, LANES), 0) == sent[index : index + 1, :], 1.0, 0.0)
        hot_r = jnp.where(iota((slots, LANES), 0) == received[index : index + 1, :], 1.0, 0.0)
        flip_out[:, rows] = hot_r.astype(NARROW)
        pad = jnp.zeros((width - 2 * slots, LANES), jnp.float32)
        both = jnp.concatenate([hot_s, hot_r, pad], axis=0)
        hot_out[rows, :] = both.T.astype(NARROW)
    for copy in copies[2:]:
        copy.wait()


def start_kernel(layer, edges, w1, w2, b1, _, start_out, w1_out, w2_out, weight, bias, w_sems):
    features = weight.shape[0]
    zeroth = fetch(b1, bias, w_sems.at[3])
    first = fetch(w1.at[layer, pl.ds(0, features), :], weight, w_sems.at[0])
    second = fetch(w1.at[layer, pl.ds(features, 2 * features), :], w1_out, w_sems.at[1])
    third = fetch(w2.at[layer], w2_out, w_sems.at[2])
    zeroth.wait()
    first.wait()
    for step in range(edges.shape[0] // ROWS):
        rows = slice(step * ROWS, (step + 1) * ROWS)
        start = dot(edges[rows, :], weight[...]) + bias[layer : layer + 1, :]
        start_out[rows, :] = (0.5 * start).astype(start_out.dtype)
    second.wait()
    third.wait()
    wide = w2_out[...].astype(jnp.float32)
    w2_out[...] = (wide - jnp.mean(wide, axis=-1, keepdims=True)).astype(NARROW)


def edge_blocks(rows):
    return [(low, low + EDGE_ROWS) for low in range(0, rows, EDGE_ROWS)]


def edge_kernel(plan, layer, hot_in, flip_in, start_in, edge_in, w1, w2, gain, shift, *refs):
    own, far_first, *refs = refs
    column_ins, refs = refs[: plan.columns - 1], refs[plan.columns - 1 :]
    edge_out, kept_out, *refs = refs
    column_outs, refs = refs[: plan.columns - 1], refs[plan.columns - 1 :]
    hidden, table = refs
    blocks = edge_blocks(edge_in.shape[0])
    steps = len(blocks)
    slots, features = plan.slots, edge_in.shape[1]
    near = plan.column_near(column_ins)
    near[0] = plan.block(own, plan.reach)
    arrived = [near[k - plan.reach] for k in range(plan.span)]
    arrived += [plan.tail(ref, plan.column_rows) for ref in (far_first, *column_ins)]
    arrived = jnp.concatenate(arrived, axis=0).astype(NARROW)
    rest = table.shape[0] - 2 * slots
    table[2 * slots :, :] = jnp.zeros((rest, features), NARROW)
    table[0:slots, :] = (0.5 * dot(arrived, w1[:features, :])).astype(NARROW)
    table[slots : 2 * slots, :] = (0.5 * dot(arrived, w1[features:, :])).astype(NARROW)

    def head(step):
        rows = slice(*blocks[step])
        half = dot(hot_in[rows, :], table[...]) + start_in[rows, :].astype(jnp.float32)
        hidden[rows, :] = silu_of_half(half).astype(NARROW)

    def tail(step):
        rows = slice(*blocks[step])
        mixed = dot(hidden[rows, :], w2[...])
        normed = scaled(mixed, gain[layer : layer + 1, :], shift[layer : layer + 1, :])
        edge_out[rows, :] = (edge_in[rows, :].astype(jnp.float32) + normed).astype(NARROW)

    for step in range(steps + 1):
        if step < steps:
            head(step)
        if step > 0:
            tail(step - 1)
    total = dot(flip_in[...], edge_out[...])
    near = {k - plan.reach: plan.block(total, k) for k in range(plan.span)}
    far = total[plan.near_total :, :]
    kept_out[...] = jnp.concatenate([near[0], far[: plan.column_rows, :]], axis=0).astype(NARROW)
    plan.column_outs(column_outs, near, far)


def node_kernel(plan, layer, last, nodes, near_table, far_table, near_in, *refs):
    line_ins, refs = refs[: plan.lines - 1], refs[plan.lines - 1 :]
    w1, b1, w2, gain, shift, node_out, *outs = refs
    states = nodes[...]
    rows, features = states.shape
    _, f = plan.here()
    summed = jnp.zeros(states.shape, jnp.float32)
    for k in range(plan.span):
        offset = k - plan.reach
        part = plan.block(near_in, k)
        if offset:
            part = jnp.where(
                plan.leaves(f, offset), plan.block(line_ins[0], abs(offset) - 1), part
            )
        summed += dot(hot(iota((rows, plan.near), 0), near_table[k]), part.astype(NARROW))
    far = [plan.tail(ref, plan.line_rows) for ref in (near_in, *line_ins)]
    picks = hot(iota((plan.far_total, rows), 1), far_rows(plan, far_table))
    summed += dot_rows(picks, jnp.concatenate(far, axis=0).astype(NARROW))
    pre = dot(states, w1[layer, :features, :])
    pre += dot(summed.astype(NARROW), w1[layer, features:, :])
    hidden = silu(pre + b1[layer : layer + 1, :]).astype(NARROW)
    mixed = dot(hidden, w2[layer])
    normed = layer_norm(mixed, gain[layer : layer + 1, :], shift[layer : layer + 1, :])
    fresh = (states.astype(jnp.float32) + normed).astype(NARROW)
    node_out[...] = fresh
    if not last:
        place(plan, fresh, near_table, picks, outs[0], outs[1:])


def cost(flops, moved):
    return pl.CostEstimate(flops=flops, bytes_accessed=moved, transcendentals=0)


def stay(array):
    return pltpu.with_memory_space_constraint(array, pltpu.HBM)


def near_by(shape):
    return pltpu.VMEM(shape, NARROW)


LOCAL = pl.BlockSpec(memory_space=pltpu.VMEM)
AWAY = pl.BlockSpec(memory_space=pl.ANY)


def call(kernel, name, limit, inputs, outputs, work, scratch=()):
    return pl.pallas_call(
        kernel,
        out_shape=[shape for _, shape in outputs],
        in_specs=[spec for spec, _ in inputs],
        out_specs=[spec for spec, _ in outputs],
        scratch_shapes=list(scratch),
        compiler_params=pltpu.CompilerParams(vmem_limit_bytes=limit << 20),
        cost_estimate=work,
        name=name,
    )(*[array for _, array in inputs])


def on_device(
    nodes,
    edges,
    near_table,
    far_table,
    edge_sender,
    edge_receiver,
    edge_w1,
    edge_b1,
    edge_w2,
    edge_gain,
    edge_shift,
    node_w1,
    node_b1,
    node_w2,
    node_gain,
    node_shift,
):
    near_table = near_table.transpose(1, 0, 2)
    far_table = far_table.transpose(0, 2, 1)
    plan = Plan(near_table.shape, far_table.shape)
    node_rows, features = nodes.shape
    edge_rows = edges.shape[0]
    layers = edge_w1.shape[0]
    hot_width = -(-2 * plan.slots // LANES) * LANES
    wide = (edge_rows, features)
    lines, columns = range(1, plan.lines), range(1, plan.columns)
    own_shape = near_by((plan.near_total + plan.line_rows, features))
    kept_shape = near_by((plan.near + plan.column_rows, features))
    far_shape = near_by((plan.column_rows, features))
    line_shapes = [near_by((plan.line_message(a), features)) for a in lines]
    column_shapes = [near_by((plan.column_message(e), features)) for e in columns]
    weight_shapes = [near_by((2 * features, features)), near_by((features, features))]

    def local(arrays):
        return [(LOCAL, array) for array in arrays]

    def away(arrays):
        return [(AWAY, stay(array)) for array in arrays]

    small = cost(4 * plan.slots * node_rows * features, 4 * plan.slots * features)
    tables = [near_table, far_table]
    own, *lines_out = call(
        functools.partial(place_kernel, plan),
        "place",
        8,
        away([nodes, *tables]),
        local([own_shape, *line_shapes]),
        small,
        [
            pltpu.VMEM(far_table.shape, jnp.int32),
            pltpu.VMEM(near_table.shape, jnp.int32),
            pltpu.VMEM(nodes.shape, NARROW),
            pltpu.SemaphoreType.DMA((3,)),
        ],
    )
    index_shape = (edge_rows // LANES, LANES)
    hot_rows, flip, edge_state, node_first, node_second = call(
        functools.partial(hots_kernel, plan),
        "hots",
        8,
        away([edge_sender.reshape(index_shape), edge_receiver.reshape(index_shape), edges])
        + away([node_w1, node_w2]),
        local([near_by((edge_rows, hot_width)), near_by((plan.slots, edge_rows)), near_by(wide)])
        + local([near_by(node_w1.shape), near_by(node_w2.shape)]),
        cost(2 * edge_rows * features * features, 8 * edge_rows * features),
        [
            pltpu.VMEM(index_shape, jnp.int32),
            pltpu.VMEM(index_shape, jnp.int32),
            pltpu.SemaphoreType.DMA((5,)),
        ],
    )
    states = nodes
    for layer in range(layers):
        last = layer == layers - 1
        lines_in = [along_node(block, a) for a, block in zip(lines, lines_out)]
        far_first, *columns_out = call(
            functools.partial(turn_out_kernel, plan),
            "turn_out",
            8,
            local([own, flip, *lines_in]),
            local([far_shape, *column_shapes]),
            small,
        )
        start, *weights = call(
            functools.partial(start_kernel, layer),
            "start",
            8,
            local([edge_state])
            + away([edge_w1, edge_w2, edge_b1])
            + local([far_first if layer == 0 else own]),
            local([near_by(wide), *weight_shapes]),
            cost(2 * edge_rows * features * features, 4 * edge_rows * features),
            [
                pltpu.VMEM((features, features), NARROW),
                pltpu.VMEM(edge_b1.shape, jnp.float32),
                pltpu.SemaphoreType.DMA((4,)),
            ],
        )
        columns_in = [along_feat(block, e) for e, block in zip(columns, columns_out)]
        scratch = [
            pltpu.VMEM(wide, NARROW),
            pltpu.VMEM((hot_width, features), NARROW),
        ]
        edge_state, kept, *columns_back = call(
            functools.partial(edge_kernel, plan, layer),
            "edge",
            16,
            local([hot_rows, flip, start, edge_state, *weights, edge_gain, edge_shift])
            + local([own, far_first, *columns_in]),
            local([near_by(wide), kept_shape, *column_shapes]),
            cost(
                2 * edge_rows * features * (hot_width + features + plan.slots),
                10 * edge_rows * features,
            ),
            scratch,
        )
        columns_in = [along_feat(block, -e) for e, block in zip(columns, columns_back)]
        near_sums, *lines_back = call(
            functools.partial(turn_back_kernel, plan),
            "turn_back",
            8,
            local([kept, *columns_in]),
            local([own_shape, *line_shapes]),
            small,
        )
        lines_in = [along_node(block, -a) for a, block in zip(lines, lines_back)]
        out_shape = [jax.ShapeDtypeStruct(nodes.shape, NARROW)] if last else [near_by(nodes.shape)]
        outs = call(
            functools.partial(node_kernel, plan, layer, last),
            "node",
            8,
            local([states, *tables, near_sums, *lines_in])
            + local([node_first, node_b1, node_second, node_gain, node_shift]),
            local(out_shape + ([] if last else [own_shape, *line_shapes])),
            small,
        )
        states = outs[0]
        if not last:
            own, *lines_out = outs[1:]
    return (states, edge_state)


def solution(mesh):
    split = ("ens", "node", "feat")
    return jax.shard_map(
        on_device,
        mesh=mesh,
        in_specs=(
            P(split, None),
            P(split, None),
            P(split, None, None),
            P(split, None, None),
            P(split),
            P(split),
        )
        + (P(),) * 10,
        out_specs=(P(split, None), P(split, None)),
        check_vma=False,
    )
```

```python
import functools

import jax
import jax.numpy as jnp
from jax import lax
from jax.experimental import pallas as pl
from jax.experimental.pallas import tpu as pltpu
from jax.sharding import PartitionSpec as P

EPSILON = 1e-05
PEERS = ("node", "feat")
ROWS = 256
EDGE_ROWS = 512
LANES = 128
NARROW = jnp.bfloat16


def grid_size():
    return lax.axis_size("node"), lax.axis_size("feat")


def side(column, columns):
    return 1 if column >= columns // 2 else -1


def along_node(block, distance):
    lines, columns = grid_size()
    route = []
    for z in range(lines):
        for f in range(columns):
            target = (z + side(f, columns) * distance) % lines
            route.append((z * columns + f, target * columns + f))
    return lax.ppermute(block, PEERS, route)


def along_feat(block, distance):
    lines, columns = grid_size()
    route = []
    for z in range(lines):
        for f in range(columns):
            route.append((z * columns + f, z * columns + (f + distance) % columns))
    return lax.ppermute(block, PEERS, route)


def dot(left, right):
    return jnp.dot(left, right, preferred_element_type=jnp.float32)


def dot_rows(left, right):
    return lax.dot_general(
        left, right, (((0,), (0,)), ((), ())), preferred_element_type=jnp.float32
    )


def silu_of_half(half):
    return half * jnp.tanh(half) + half


def silu(values):
    return silu_of_half(0.5 * values)


def layer_norm(values, norm_gain, norm_shift):
    center = values - jnp.mean(values, axis=-1, keepdims=True)
    return scaled(center, norm_gain, norm_shift)


def scaled(center, norm_gain, norm_shift):
    spread = jnp.mean(center * center, axis=-1, keepdims=True)
    return center * lax.rsqrt(spread + EPSILON) * norm_gain + norm_shift


def iota(shape, axis):
    return lax.broadcasted_iota(jnp.int32, shape, axis)


def hot(left, right):
    return jnp.where(left == right, 1.0, 0.0).astype(NARROW)


class Plan:
    def __init__(self, near_shape, far_shape):
        self.lines, self.columns = grid_size()
        self.span, _, self.near = near_shape
        self.reach = (self.span - 1) // 2
        self.width = far_shape[1]
        self.line_rows = self.columns * self.width
        self.column_rows = self.lines * self.width
        self.near_total = self.span * self.near
        self.far_total = self.lines * self.line_rows
        self.slots = self.near_total + self.far_total
        self.offsets = [o for o in range(-self.reach, self.reach + 1) if o]

    def here(self):
        return lax.axis_index("node"), lax.axis_index("feat")

    def upper(self, column):
        return column >= self.columns // 2

    def leaves(self, column, offset):
        return jnp.logical_or(column + offset < 0, column + offset >= self.columns)

    def near_in(self, e):
        return [o for o in self.offsets if o % self.columns == e]

    def line_message(self, a):
        return (self.reach * self.near if a == 1 else 0) + self.line_rows

    def column_message(self, e):
        return len(self.near_in(e)) * self.near + self.column_rows

    def block(self, ref, index):
        return ref[index * self.near : (index + 1) * self.near, :].astype(jnp.float32)

    def tail(self, ref, count):
        rows = ref.shape[0]
        return ref[rows - count : rows, :].astype(jnp.float32)

    def line_outs(self, outs, near, far, column):
        for a, out in enumerate(outs, 1):
            parts = [far[a * self.line_rows : (a + 1) * self.line_rows, :]]
            if a == 1:
                upper = self.upper(column)
                relayed = [
                    jnp.where(upper, near[i], near[-i]) for i in range(1, self.reach + 1)
                ]
                parts = relayed + parts
            out[...] = jnp.concatenate(parts, axis=0).astype(out.dtype)

    def column_outs(self, outs, near, far):
        for e, out in enumerate(outs, 1):
            parts = [near[o] for o in self.near_in(e)]
            parts.append(far[e * self.column_rows : (e + 1) * self.column_rows, :])
            out[...] = jnp.concatenate(parts, axis=0).astype(out.dtype)

    def column_near(self, ins):
        near = {}
        for e, ref in enumerate(ins, 1):
            for i, o in enumerate(self.near_in(e)):
                near[o] = self.block(ref, i)
        return near

    def reorder(self, far, outer):
        total = self.far_total
        inner = total // (outer * self.width)
        row = iota((total, total), 0)
        c, rest = row % self.width, row // self.width
        source = ((rest % outer) * inner + rest // outer) * self.width + c
        return dot(hot(iota((total, total), 1), source), far.astype(NARROW))


def far_rows(plan, far_ref):
    z, f = plan.here()
    table = far_ref[0].astype(jnp.float32)
    width, peers = table.shape
    total = peers * width
    row = iota((total, peers), 0)
    e = (row // width) % plan.columns
    a = row // plan.line_rows
    a = jnp.where(plan.upper(f), a, plan.lines - a)
    peer = ((z + a) % plan.lines) * plan.columns + (f + e) % plan.columns
    spread = jnp.where(peer == iota((total, peers), 1), 1.0, 0.0)
    wide = lax.dot_general(
        spread,
        table,
        (((1,), (1,)), ((), ())),
        preferred_element_type=jnp.float32,
        precision=lax.Precision.HIGHEST,
    )
    own = iota((total, width), 0) % width == iota((total, width), 1)
    return jnp.sum(jnp.where(own, wide, 0.0), axis=1, keepdims=True).astype(jnp.int32)


def place(plan, near, far, own_out, line_outs):
    own = [near[k - plan.reach] for k in range(plan.span)] + [far[: plan.line_rows, :]]
    own_out[...] = jnp.concatenate(own, axis=0).astype(own_out.dtype)
    plan.line_outs(line_outs, near, far, plan.here()[1])


def place_kernel(plan, nodes, near, far, own_out, *refs):
    line_outs, held = refs[: plan.lines - 1], refs[plan.lines - 1 : -1]
    copies = [fetch(a, b, refs[-1].at[i]) for i, (a, b) in enumerate(zip((far, near, nodes), held))]
    far_held, near_held, states = held
    rows = states.shape[0]
    copies[0].wait()
    picks = hot(iota((plan.far_total, rows), 1), far_rows(plan, far_held))
    for copy in copies[1:]:
        copy.wait()
    here = states[...]
    placed = {}
    for k in range(plan.span):
        placed[k - plan.reach] = dot_rows(hot(iota((rows, plan.near), 0), near_held[k]), here)
    place(plan, placed, dot(picks, here), own_out, line_outs)


def turn_out_kernel(plan, own, _, *refs):
    line_ins, far_out = refs[: plan.lines - 1], refs[plan.lines - 1]
    column_outs = refs[plan.lines :]
    _, f = plan.here()
    near = {}
    for o in plan.offsets:
        mine = plan.block(own, o + plan.reach)
        near[o] = jnp.where(plan.leaves(f, o), plan.block(line_ins[0], abs(o) - 1), mine)
    far = [plan.tail(ref, plan.line_rows) for ref in (own, *line_ins)]
    far = plan.reorder(jnp.concatenate(far, axis=0), plan.lines)
    far_out[...] = far[: plan.column_rows, :].astype(far_out.dtype)
    plan.column_outs(column_outs, near, far)


def turn_back_kernel(plan, kept, *refs):
    column_ins, near_out = refs[: plan.columns - 1], refs[plan.columns - 1]
    line_outs = refs[plan.columns :]
    _, f = plan.here()
    near = plan.column_near(column_ins)
    near[0] = plan.block(kept, 0)
    far = [plan.tail(ref, plan.column_rows) for ref in (kept, *column_ins)]
    far = plan.reorder(jnp.concatenate(far, axis=0), plan.columns)
    own = [near[k - plan.reach] for k in range(plan.span)] + [far[: plan.line_rows, :]]
    near_out[...] = jnp.concatenate(own, axis=0).astype(near_out.dtype)
    plan.line_outs(line_outs, near, far, f)


def fetch(source, target, sem):
    copy = pltpu.make_async_copy(source, target, sem)
    copy.start()
    return copy


def in_order(plan, slot):
    z, f = plan.here()
    t = jnp.maximum(slot - plan.near_total, 0)
    c, p = t % plan.width, t // plan.width
    line, column = p // plan.columns, p % plan.columns
    e = (f - column + plan.columns) % plan.columns
    away = jnp.where(plan.upper(column), z - line, line - z)
    a = (away + plan.lines) % plan.lines
    renamed = plan.near_total + (e * plan.lines + a) * plan.width + c
    return jnp.where(slot < plan.near_total, slot, renamed)


def hots_kernel(plan, sender, receiver, edges, w1, w2, near, far, *refs):
    hot_out, flip_out, edge_out, w1_out, w2_out, pick_out, gather_out, *refs = refs
    near_held, far_held, sender_held, receiver_held, sems = refs
    slots = plan.slots
    edge_rows, width = hot_out.shape
    copies = [
        fetch(sender, sender_held, sems.at[0]),
        fetch(receiver, receiver_held, sems.at[1]),
        fetch(edges, edge_out, sems.at[2]),
        fetch(w1, w1_out, sems.at[3]),
        fetch(w2, w2_out, sems.at[4]),
        fetch(near, near_held, sems.at[5]),
        fetch(far, far_held, sems.at[6]),
    ]
    copies[0].wait()
    copies[1].wait()
    sent = in_order(plan, sender_held[...])
    received = in_order(plan, receiver_held[...])
    for index in range(edge_rows // LANES):
        rows = slice(index * LANES, (index + 1) * LANES)
        hot_s = jnp.where(iota((slots, LANES), 0) == sent[index : index + 1, :], 1.0, 0.0)
        hot_r = jnp.where(iota((slots, LANES), 0) == received[index : index + 1, :], 1.0, 0.0)
        flip_out[:, rows] = hot_r.astype(NARROW)
        pad = jnp.zeros((width - 2 * slots, LANES), jnp.float32)
        both = jnp.concatenate([hot_s, hot_r, pad], axis=0)
        hot_out[rows, :] = both.T.astype(NARROW)
    for copy in copies[2:]:
        copy.wait()
    node_rows = pick_out.shape[0]
    near_rows = [hot(iota((node_rows, plan.near), 0), near_held[k]) for k in range(plan.span)]
    far_picks = hot(iota((plan.far_total, node_rows), 1), far_rows(plan, far_held))
    flipped = [block.astype(jnp.float32).T for block in near_rows]
    flipped = jnp.concatenate(flipped + [far_picks.astype(jnp.float32)], axis=0)
    gather_out[...] = flipped.astype(NARROW)
    pick_out[...] = flipped.T.astype(NARROW)


def start_kernel(layer, edges, w1, w2, b1, _, start_out, w1_out, w2_out, weight, bias, w_sems):
    features = weight.shape[0]
    zeroth = fetch(b1, bias, w_sems.at[3])
    first = fetch(w1.at[layer, pl.ds(0, features), :], weight, w_sems.at[0])
    second = fetch(w1.at[layer, pl.ds(features, 2 * features), :], w1_out, w_sems.at[1])
    third = fetch(w2.at[layer], w2_out, w_sems.at[2])
    zeroth.wait()
    first.wait()
    for step in range(edges.shape[0] // ROWS):
        rows = slice(step * ROWS, (step + 1) * ROWS)
        start = dot(edges[rows, :], weight[...]) + bias[layer : layer + 1, :]
        start_out[rows, :] = (0.5 * start).astype(start_out.dtype)
    second.wait()
    third.wait()
    wide = w2_out[...].astype(jnp.float32)
    w2_out[...] = (wide - jnp.mean(wide, axis=-1, keepdims=True)).astype(NARROW)


def edge_blocks(rows):
    return [(low, low + EDGE_ROWS) for low in range(0, rows, EDGE_ROWS)]


def edge_kernel(plan, layer, hot_in, flip_in, start_in, edge_in, w1, w2, gain, shift, *refs):
    own, far_first, *refs = refs
    column_ins, refs = refs[: plan.columns - 1], refs[plan.columns - 1 :]
    edge_out, kept_out, *refs = refs
    column_outs, refs = refs[: plan.columns - 1], refs[plan.columns - 1 :]
    hidden, table = refs
    blocks = edge_blocks(edge_in.shape[0])
    steps = len(blocks)
    slots, features = plan.slots, edge_in.shape[1]
    near = plan.column_near(column_ins)
    near[0] = plan.block(own, plan.reach)
    arrived = [near[k - plan.reach] for k in range(plan.span)]
    arrived += [plan.tail(ref, plan.column_rows) for ref in (far_first, *column_ins)]
    arrived = jnp.concatenate(arrived, axis=0).astype(NARROW)
    rest = table.shape[0] - 2 * slots
    table[2 * slots :, :] = jnp.zeros((rest, features), NARROW)
    table[0:slots, :] = (0.5 * dot(arrived, w1[:features, :])).astype(NARROW)
    table[slots : 2 * slots, :] = (0.5 * dot(arrived, w1[features:, :])).astype(NARROW)

    def head(step):
        rows = slice(*blocks[step])
        half = dot(hot_in[rows, :], table[...]) + start_in[rows, :].astype(jnp.float32)
        hidden[rows, :] = silu_of_half(half).astype(NARROW)

    def tail(step):
        rows = slice(*blocks[step])
        mixed = dot(hidden[rows, :], w2[...])
        normed = scaled(mixed, gain[layer : layer + 1, :], shift[layer : layer + 1, :])
        edge_out[rows, :] = (edge_in[rows, :].astype(jnp.float32) + normed).astype(NARROW)

    for step in range(steps + 1):
        if step < steps:
            head(step)
        if step > 0:
            tail(step - 1)
    total = dot(flip_in[...], edge_out[...])
    near = {k - plan.reach: plan.block(total, k) for k in range(plan.span)}
    far = total[plan.near_total :, :]
    kept_out[...] = jnp.concatenate([near[0], far[: plan.column_rows, :]], axis=0).astype(NARROW)
    plan.column_outs(column_outs, near, far)


def node_kernel(plan, layer, last, nodes, picks, gather, near_in, *refs):
    line_ins, refs = refs[: plan.lines - 1], refs[plan.lines - 1 :]
    w1, b1, w2, gain, shift, node_out, *outs = refs
    states = nodes[...]
    features = states.shape[1]
    _, f = plan.here()
    parts = []
    for k in range(plan.span):
        offset = k - plan.reach
        part = plan.block(near_in, k)
        if offset:
            part = jnp.where(
                plan.leaves(f, offset), plan.block(line_ins[0], abs(offset) - 1), part
            )
        parts.append(part)
    parts += [plan.tail(ref, plan.line_rows) for ref in (near_in, *line_ins)]
    summed = dot(picks[...], jnp.concatenate(parts, axis=0).astype(NARROW))
    pre = dot(states, w1[layer, :features, :])
    pre += dot(summed.astype(NARROW), w1[layer, features:, :])
    hidden = silu(pre + b1[layer : layer + 1, :]).astype(NARROW)
    mixed = dot(hidden, w2[layer])
    normed = layer_norm(mixed, gain[layer : layer + 1, :], shift[layer : layer + 1, :])
    fresh = (states.astype(jnp.float32) + normed).astype(NARROW)
    node_out[...] = fresh
    if not last:
        placed = dot(gather[...], fresh)
        near = {k - plan.reach: plan.block(placed, k) for k in range(plan.span)}
        place(plan, near, placed[plan.near_total :, :], outs[0], outs[1:])


def cost(flops, moved):
    return pl.CostEstimate(flops=flops, bytes_accessed=moved, transcendentals=0)


def stay(array):
    return pltpu.with_memory_space_constraint(array, pltpu.HBM)


def near_by(shape):
    return pltpu.VMEM(shape, NARROW)


LOCAL = pl.BlockSpec(memory_space=pltpu.VMEM)
AWAY = pl.BlockSpec(memory_space=pl.ANY)


def call(kernel, name, limit, inputs, outputs, work, scratch=()):
    return pl.pallas_call(
        kernel,
        out_shape=[shape for _, shape in outputs],
        in_specs=[spec for spec, _ in inputs],
        out_specs=[spec for spec, _ in outputs],
        scratch_shapes=list(scratch),
        compiler_params=pltpu.CompilerParams(vmem_limit_bytes=limit << 20),
        cost_estimate=work,
        name=name,
    )(*[array for _, array in inputs])


def on_device(
    nodes,
    edges,
    near_table,
    far_table,
    edge_sender,
    edge_receiver,
    edge_w1,
    edge_b1,
    edge_w2,
    edge_gain,
    edge_shift,
    node_w1,
    node_b1,
    node_w2,
    node_gain,
    node_shift,
):
    near_table = near_table.transpose(1, 0, 2)
    far_table = far_table.transpose(0, 2, 1)
    plan = Plan(near_table.shape, far_table.shape)
    node_rows, features = nodes.shape
    edge_rows = edges.shape[0]
    layers = edge_w1.shape[0]
    hot_width = -(-2 * plan.slots // LANES) * LANES
    wide = (edge_rows, features)
    lines, columns = range(1, plan.lines), range(1, plan.columns)
    own_shape = near_by((plan.near_total + plan.line_rows, features))
    kept_shape = near_by((plan.near + plan.column_rows, features))
    far_shape = near_by((plan.column_rows, features))
    line_shapes = [near_by((plan.line_message(a), features)) for a in lines]
    column_shapes = [near_by((plan.column_message(e), features)) for e in columns]
    weight_shapes = [near_by((2 * features, features)), near_by((features, features))]

    def local(arrays):
        return [(LOCAL, array) for array in arrays]

    def away(arrays):
        return [(AWAY, stay(array)) for array in arrays]

    small = cost(4 * plan.slots * node_rows * features, 4 * plan.slots * features)
    tables = [near_table, far_table]
    own, *lines_out = call(
        functools.partial(place_kernel, plan),
        "place",
        8,
        away([nodes, *tables]),
        local([own_shape, *line_shapes]),
        small,
        [
            pltpu.VMEM(far_table.shape, jnp.int32),
            pltpu.VMEM(near_table.shape, jnp.int32),
            pltpu.VMEM(nodes.shape, NARROW),
            pltpu.SemaphoreType.DMA((3,)),
        ],
    )
    index_shape = (edge_rows // LANES, LANES)
    hot_rows, flip, edge_state, node_first, node_second, *selections = call(
        functools.partial(hots_kernel, plan),
        "hots",
        8,
        away([edge_sender.reshape(index_shape), edge_receiver.reshape(index_shape), edges])
        + away([node_w1, node_w2, *tables]),
        local([near_by((edge_rows, hot_width)), near_by((plan.slots, edge_rows)), near_by(wide)])
        + local([near_by(node_w1.shape), near_by(node_w2.shape)])
        + local([near_by((node_rows, plan.slots)), near_by((plan.slots, node_rows))]),
        cost(2 * edge_rows * features * features, 8 * edge_rows * features),
        [
            pltpu.VMEM(near_table.shape, jnp.int32),
            pltpu.VMEM(far_table.shape, jnp.int32),
            pltpu.VMEM(index_shape, jnp.int32),
            pltpu.VMEM(index_shape, jnp.int32),
            pltpu.SemaphoreType.DMA((7,)),
        ],
    )
    states = nodes
    for layer in range(layers):
        last = layer == layers - 1
        lines_in = [along_node(block, a) for a, block in zip(lines, lines_out)]
        far_first, *columns_out = call(
            functools.partial(turn_out_kernel, plan),
            "turn_out",
            8,
            local([own, flip, *lines_in]),
            local([far_shape, *column_shapes]),
            small,
        )
        start, *weights = call(
            functools.partial(start_kernel, layer),
            "start",
            8,
            local([edge_state])
            + away([edge_w1, edge_w2, edge_b1])
            + local([far_first if layer == 0 else own]),
            local([near_by(wide), *weight_shapes]),
            cost(2 * edge_rows * features * features, 4 * edge_rows * features),
            [
                pltpu.VMEM((features, features), NARROW),
                pltpu.VMEM(edge_b1.shape, jnp.float32),
                pltpu.SemaphoreType.DMA((4,)),
            ],
        )
        columns_in = [along_feat(block, e) for e, block in zip(columns, columns_out)]
        scratch = [
            pltpu.VMEM(wide, NARROW),
            pltpu.VMEM((hot_width, features), NARROW),
        ]
        edge_state, kept, *columns_back = call(
            functools.partial(edge_kernel, plan, layer),
            "edge",
            16,
            local([hot_rows, flip, start, edge_state, *weights, edge_gain, edge_shift])
            + local([own, far_first, *columns_in]),
            local([near_by(wide), kept_shape, *column_shapes]),
            cost(
                2 * edge_rows * features * (hot_width + features + plan.slots),
                10 * edge_rows * features,
            ),
            scratch,
        )
        columns_in = [along_feat(block, -e) for e, block in zip(columns, columns_back)]
        near_sums, *lines_back = call(
            functools.partial(turn_back_kernel, plan),
            "turn_back",
            8,
            local([kept, *columns_in]),
            local([own_shape, *line_shapes]),
            small,
        )
        lines_in = [along_node(block, -a) for a, block in zip(lines, lines_back)]
        out_shape = [jax.ShapeDtypeStruct(nodes.shape, NARROW)] if last else [near_by(nodes.shape)]
        outs = call(
            functools.partial(node_kernel, plan, layer, last),
            "node",
            8,
            local([states, *selections, near_sums, *lines_in])
            + local([node_first, node_b1, node_second, node_gain, node_shift]),
            local(out_shape + ([] if last else [own_shape, *line_shapes])),
            small,
        )
        states = outs[0]
        if not last:
            own, *lines_out = outs[1:]
    return (states, edge_state)


def solution(mesh):
    split = ("ens", "node", "feat")
    return jax.shard_map(
        on_device,
        mesh=mesh,
        in_specs=(
            P(split, None),
            P(split, None),
            P(split, None, None),
            P(split, None, None),
            P(split),
            P(split),
        )
        + (P(),) * 10,
        out_specs=(P(split, None), P(split, None)),
        check_vma=False,
    )
```

```python
import functools

import jax
import jax.numpy as jnp
from jax import lax
from jax.experimental import pallas as pl
from jax.experimental.pallas import tpu as pltpu
from jax.sharding import PartitionSpec as P

EPSILON = 1e-05
PEERS = ("node", "feat")
ROWS = 256
EDGE_ROWS = 512
LANES = 128
NARROW = jnp.bfloat16


def grid_size():
    return lax.axis_size("node"), lax.axis_size("feat")


def side(column, columns):
    return 1 if column >= columns // 2 else -1


def along_node(block, distance):
    lines, columns = grid_size()
    route = []
    for z in range(lines):
        for f in range(columns):
            target = (z + side(f, columns) * distance) % lines
            route.append((z * columns + f, target * columns + f))
    return lax.ppermute(block, PEERS, route)


def along_feat(block, distance):
    lines, columns = grid_size()
    route = []
    for z in range(lines):
        for f in range(columns):
            route.append((z * columns + f, z * columns + (f + distance) % columns))
    return lax.ppermute(block, PEERS, route)


def dot(left, right):
    return jnp.dot(left, right, preferred_element_type=jnp.float32)


def dot_rows(left, right):
    return lax.dot_general(
        left, right, (((0,), (0,)), ((), ())), preferred_element_type=jnp.float32
    )


def silu_of_half(half):
    return half * jnp.tanh(half) + half


def silu(values):
    return silu_of_half(0.5 * values)


def layer_norm(values, norm_gain, norm_shift):
    center = values - jnp.mean(values, axis=-1, keepdims=True)
    return scaled(center, norm_gain, norm_shift)


def scaled(center, norm_gain, norm_shift):
    spread = jnp.mean(center * center, axis=-1, keepdims=True)
    return center * lax.rsqrt(spread + EPSILON) * norm_gain + norm_shift


def iota(shape, axis):
    return lax.broadcasted_iota(jnp.int32, shape, axis)


def hot(left, right):
    return jnp.where(left == right, 1.0, 0.0).astype(NARROW)


class Plan:
    def __init__(self, near_shape, far_shape):
        self.lines, self.columns = grid_size()
        self.span, _, self.near = near_shape
        self.reach = (self.span - 1) // 2
        self.width = far_shape[1]
        self.line_rows = self.columns * self.width
        self.column_rows = self.lines * self.width
        self.near_total = self.span * self.near
        self.far_total = self.lines * self.line_rows
        self.slots = self.near_total + self.far_total
        self.others = self.slots - self.near
        self.own_rows = slice(self.reach * self.near, (self.reach + 1) * self.near)
        self.offsets = [o for o in range(-self.reach, self.reach + 1) if o]

    def here(self):
        return lax.axis_index("node"), lax.axis_index("feat")

    def upper(self, column):
        return column >= self.columns // 2

    def leaves(self, column, offset):
        return jnp.logical_or(column + offset < 0, column + offset >= self.columns)

    def near_in(self, e):
        return [o for o in self.offsets if o % self.columns == e]

    def line_message(self, a):
        return (self.reach * self.near if a == 1 else 0) + self.line_rows

    def column_message(self, e):
        return len(self.near_in(e)) * self.near + self.column_rows

    def part_own(self, rows):
        low, high = self.own_rows.start, self.own_rows.stop
        return rows[low:high, :], jnp.concatenate([rows[:low, :], rows[high:, :]], axis=0)

    def block(self, ref, index):
        return ref[index * self.near : (index + 1) * self.near, :].astype(jnp.float32)

    def tail(self, ref, count):
        rows = ref.shape[0]
        return ref[rows - count : rows, :].astype(jnp.float32)

    def line_outs(self, outs, near, far, column):
        for a, out in enumerate(outs, 1):
            parts = [far[a * self.line_rows : (a + 1) * self.line_rows, :]]
            if a == 1:
                upper = self.upper(column)
                relayed = [
                    jnp.where(upper, near[i], near[-i]) for i in range(1, self.reach + 1)
                ]
                parts = relayed + parts
            out[...] = jnp.concatenate(parts, axis=0).astype(out.dtype)

    def column_outs(self, outs, near, far):
        for e, out in enumerate(outs, 1):
            parts = [near[o] for o in self.near_in(e)]
            parts.append(far[e * self.column_rows : (e + 1) * self.column_rows, :])
            out[...] = jnp.concatenate(parts, axis=0).astype(out.dtype)

    def column_near(self, ins):
        near = {}
        for e, ref in enumerate(ins, 1):
            for i, o in enumerate(self.near_in(e)):
                near[o] = self.block(ref, i)
        return near

    def reorder(self, far, outer):
        total = self.far_total
        inner = total // (outer * self.width)
        row = iota((total, total), 0)
        c, rest = row % self.width, row // self.width
        source = ((rest % outer) * inner + rest // outer) * self.width + c
        return dot(hot(iota((total, total), 1), source), far.astype(NARROW))


def far_rows(plan, far_ref):
    z, f = plan.here()
    table = far_ref[0].astype(jnp.float32)
    width, peers = table.shape
    total = peers * width
    row = iota((total, peers), 0)
    e = (row // width) % plan.columns
    a = row // plan.line_rows
    a = jnp.where(plan.upper(f), a, plan.lines - a)
    peer = ((z + a) % plan.lines) * plan.columns + (f + e) % plan.columns
    spread = jnp.where(peer == iota((total, peers), 1), 1.0, 0.0)
    wide = lax.dot_general(
        spread,
        table,
        (((1,), (1,)), ((), ())),
        preferred_element_type=jnp.float32,
        precision=lax.Precision.HIGHEST,
    )
    own = iota((total, width), 0) % width == iota((total, width), 1)
    return jnp.sum(jnp.where(own, wide, 0.0), axis=1, keepdims=True).astype(jnp.int32)


def place(plan, near, far, own_out, line_outs):
    own = [near[k - plan.reach] for k in range(plan.span)] + [far[: plan.line_rows, :]]
    own_out[...] = jnp.concatenate(own, axis=0).astype(own_out.dtype)
    plan.line_outs(line_outs, near, far, plan.here()[1])


def place_kernel(plan, nodes, near, far, own_out, *refs):
    line_outs, held = refs[: plan.lines - 1], refs[plan.lines - 1 : -1]
    copies = [fetch(a, b, refs[-1].at[i]) for i, (a, b) in enumerate(zip((far, near, nodes), held))]
    far_held, near_held, states = held
    rows = states.shape[0]
    copies[0].wait()
    picks = hot(iota((plan.far_total, rows), 1), far_rows(plan, far_held))
    for copy in copies[1:]:
        copy.wait()
    here = states[...]
    placed = {}
    for k in range(plan.span):
        placed[k - plan.reach] = dot_rows(hot(iota((rows, plan.near), 0), near_held[k]), here)
    place(plan, placed, dot(picks, here), own_out, line_outs)


def turn_out_kernel(plan, own, _, *refs):
    line_ins, far_out = refs[: plan.lines - 1], refs[plan.lines - 1]
    column_outs = refs[plan.lines :]
    _, f = plan.here()
    near = {}
    for o in plan.offsets:
        mine = plan.block(own, o + plan.reach)
        near[o] = jnp.where(plan.leaves(f, o), plan.block(line_ins[0], abs(o) - 1), mine)
    far = [plan.tail(ref, plan.line_rows) for ref in (own, *line_ins)]
    far = plan.reorder(jnp.concatenate(far, axis=0), plan.lines)
    far_out[...] = far[: plan.column_rows, :].astype(far_out.dtype)
    plan.column_outs(column_outs, near, far)


def turn_back_kernel(plan, kept, *refs):
    column_ins, near_out = refs[: plan.columns - 1], refs[plan.columns - 1]
    line_outs = refs[plan.columns :]
    _, f = plan.here()
    near = plan.column_near(column_ins)
    near[0] = plan.block(kept, 0)
    far = [plan.tail(ref, plan.column_rows) for ref in (kept, *column_ins)]
    far = plan.reorder(jnp.concatenate(far, axis=0), plan.columns)
    own = [near[k - plan.reach] for k in range(plan.span)] + [far[: plan.line_rows, :]]
    near_out[...] = jnp.concatenate(own, axis=0).astype(near_out.dtype)
    plan.line_outs(line_outs, near, far, f)


def fetch(source, target, sem):
    copy = pltpu.make_async_copy(source, target, sem)
    copy.start()
    return copy


def in_order(plan, slot):
    z, f = plan.here()
    t = jnp.maximum(slot - plan.near_total, 0)
    c, p = t % plan.width, t // plan.width
    line, column = p // plan.columns, p % plan.columns
    e = (f - column + plan.columns) % plan.columns
    away = jnp.where(plan.upper(column), z - line, line - z)
    a = (away + plan.lines) % plan.lines
    renamed = plan.near_total + (e * plan.lines + a) * plan.width + c
    return jnp.where(slot < plan.near_total, slot, renamed)


def hots_kernel(plan, sender, receiver, edges, w1, w2, near, far, *refs):
    hot_out, own_hot_out, flip_out, edge_out, w1_out, w2_out, pick_out, gather_out, *refs = refs
    near_held, far_held, sender_held, receiver_held, sems = refs
    slots = plan.slots
    edge_rows = hot_out.shape[0]
    copies = [
        fetch(sender, sender_held, sems.at[0]),
        fetch(receiver, receiver_held, sems.at[1]),
        fetch(edges, edge_out, sems.at[2]),
        fetch(w1, w1_out, sems.at[3]),
        fetch(w2, w2_out, sems.at[4]),
        fetch(near, near_held, sems.at[5]),
        fetch(far, far_held, sems.at[6]),
    ]
    copies[0].wait()
    copies[1].wait()
    sent = in_order(plan, sender_held[...])
    received = in_order(plan, receiver_held[...])
    for index in range(edge_rows // LANES):
        rows = slice(index * LANES, (index + 1) * LANES)
        hot_s = jnp.where(iota((slots, LANES), 0) == sent[index : index + 1, :], 1.0, 0.0)
        hot_r = jnp.where(iota((slots, LANES), 0) == received[index : index + 1, :], 1.0, 0.0)
        flip_out[:, rows] = hot_r.astype(NARROW)
        own, others = zip(plan.part_own(hot_s), plan.part_own(hot_r))
        for parts, out in ((own, own_hot_out), (others, hot_out)):
            count = out.shape[1] - 2 * parts[0].shape[0]
            pad = [jnp.zeros((count, LANES), jnp.float32)] if count else []
            out[rows, :] = jnp.concatenate([*parts, *pad], axis=0).T.astype(NARROW)
    for copy in copies[2:]:
        copy.wait()
    node_rows = pick_out.shape[0]
    near_rows = [hot(iota((node_rows, plan.near), 0), near_held[k]) for k in range(plan.span)]
    far_picks = hot(iota((plan.far_total, node_rows), 1), far_rows(plan, far_held))
    flipped = [block.astype(jnp.float32).T for block in near_rows]
    flipped = jnp.concatenate(flipped + [far_picks.astype(jnp.float32)], axis=0)
    gather_out[...] = flipped.astype(NARROW)
    pick_out[...] = flipped.T.astype(NARROW)


def start_kernel(plan, layer, edges, own_hot, own, w1, w2, b1, _, start_out, *refs):
    w1_out, w2_out, weight, bias, table, w_sems = refs
    features = weight.shape[0]
    zeroth = fetch(b1, bias, w_sems.at[3])
    first = fetch(w1.at[layer, pl.ds(0, features), :], weight, w_sems.at[0])
    second = fetch(w1.at[layer, pl.ds(features, 2 * features), :], w1_out, w_sems.at[1])
    third = fetch(w2.at[layer], w2_out, w_sems.at[2])
    zeroth.wait()
    first.wait()
    second.wait()
    rows = own[plan.own_rows, :]
    tables = [0.5 * dot(rows, w1_out[:features, :]), 0.5 * dot(rows, w1_out[features:, :])]
    count = table.shape[0] - 2 * plan.near
    if count:
        tables.append(jnp.zeros((count, features), jnp.float32))
    table[...] = jnp.concatenate(tables, axis=0).astype(NARROW)
    for step in range(edges.shape[0] // ROWS):
        rows = slice(step * ROWS, (step + 1) * ROWS)
        start = dot(edges[rows, :], weight[...]) + bias[layer : layer + 1, :]
        start = 0.5 * start + dot(own_hot[rows, :], table[...])
        start_out[rows, :] = start.astype(start_out.dtype)
    third.wait()
    wide = w2_out[...].astype(jnp.float32)
    w2_out[...] = (wide - jnp.mean(wide, axis=-1, keepdims=True)).astype(NARROW)


def edge_blocks(rows):
    return [(low, low + EDGE_ROWS) for low in range(0, rows, EDGE_ROWS)]


def edge_kernel(plan, layer, hot_in, flip_in, start_in, edge_in, w1, w2, gain, shift, *refs):
    far_first, *refs = refs
    column_ins, refs = refs[: plan.columns - 1], refs[plan.columns - 1 :]
    edge_out, kept_out, *refs = refs
    column_outs, refs = refs[: plan.columns - 1], refs[plan.columns - 1 :]
    hidden, table = refs
    blocks = edge_blocks(edge_in.shape[0])
    steps = len(blocks)
    slots, features = plan.others, edge_in.shape[1]
    near = plan.column_near(column_ins)
    arrived = [near[o] for o in plan.offsets]
    arrived += [plan.tail(ref, plan.column_rows) for ref in (far_first, *column_ins)]
    arrived = jnp.concatenate(arrived, axis=0).astype(NARROW)
    rest = table.shape[0] - 2 * slots
    if rest:
        table[2 * slots :, :] = jnp.zeros((rest, features), NARROW)
    table[0:slots, :] = (0.5 * dot(arrived, w1[:features, :])).astype(NARROW)
    table[slots : 2 * slots, :] = (0.5 * dot(arrived, w1[features:, :])).astype(NARROW)

    def head(step):
        rows = slice(*blocks[step])
        half = dot(hot_in[rows, :], table[...]) + start_in[rows, :].astype(jnp.float32)
        hidden[rows, :] = silu_of_half(half).astype(NARROW)

    def tail(step):
        rows = slice(*blocks[step])
        mixed = dot(hidden[rows, :], w2[...])
        normed = scaled(mixed, gain[layer : layer + 1, :], shift[layer : layer + 1, :])
        edge_out[rows, :] = (edge_in[rows, :].astype(jnp.float32) + normed).astype(NARROW)

    for step in range(steps + 1):
        if step < steps:
            head(step)
        if step > 0:
            tail(step - 1)
    total = dot(flip_in[...], edge_out[...])
    near = {k - plan.reach: plan.block(total, k) for k in range(plan.span)}
    far = total[plan.near_total :, :]
    kept_out[...] = jnp.concatenate([near[0], far[: plan.column_rows, :]], axis=0).astype(NARROW)
    plan.column_outs(column_outs, near, far)


def node_kernel(plan, layer, last, nodes, picks, gather, near_in, *refs):
    line_ins, refs = refs[: plan.lines - 1], refs[plan.lines - 1 :]
    w1, b1, w2, gain, shift, node_out, *outs = refs
    states = nodes[...]
    features = states.shape[1]
    _, f = plan.here()
    parts = []
    for k in range(plan.span):
        offset = k - plan.reach
        part = plan.block(near_in, k)
        if offset:
            part = jnp.where(
                plan.leaves(f, offset), plan.block(line_ins[0], abs(offset) - 1), part
            )
        parts.append(part)
    parts += [plan.tail(ref, plan.line_rows) for ref in (near_in, *line_ins)]
    summed = dot(picks[...], jnp.concatenate(parts, axis=0).astype(NARROW))
    pre = dot(states, w1[layer, :features, :])
    pre += dot(summed.astype(NARROW), w1[layer, features:, :])
    hidden = silu(pre + b1[layer : layer + 1, :]).astype(NARROW)
    mixed = dot(hidden, w2[layer])
    normed = layer_norm(mixed, gain[layer : layer + 1, :], shift[layer : layer + 1, :])
    fresh = (states.astype(jnp.float32) + normed).astype(NARROW)
    node_out[...] = fresh
    if not last:
        placed = dot(gather[...], fresh)
        near = {k - plan.reach: plan.block(placed, k) for k in range(plan.span)}
        place(plan, near, placed[plan.near_total :, :], outs[0], outs[1:])


def cost(flops, moved):
    return pl.CostEstimate(flops=flops, bytes_accessed=moved, transcendentals=0)


def stay(array):
    return pltpu.with_memory_space_constraint(array, pltpu.HBM)


def near_by(shape):
    return pltpu.VMEM(shape, NARROW)


LOCAL = pl.BlockSpec(memory_space=pltpu.VMEM)
AWAY = pl.BlockSpec(memory_space=pl.ANY)


def call(kernel, name, limit, inputs, outputs, work, scratch=()):
    return pl.pallas_call(
        kernel,
        out_shape=[shape for _, shape in outputs],
        in_specs=[spec for spec, _ in inputs],
        out_specs=[spec for spec, _ in outputs],
        scratch_shapes=list(scratch),
        compiler_params=pltpu.CompilerParams(vmem_limit_bytes=limit << 20),
        cost_estimate=work,
        name=name,
    )(*[array for _, array in inputs])


def on_device(
    nodes,
    edges,
    near_table,
    far_table,
    edge_sender,
    edge_receiver,
    edge_w1,
    edge_b1,
    edge_w2,
    edge_gain,
    edge_shift,
    node_w1,
    node_b1,
    node_w2,
    node_gain,
    node_shift,
):
    near_table = near_table.transpose(1, 0, 2)
    far_table = far_table.transpose(0, 2, 1)
    plan = Plan(near_table.shape, far_table.shape)
    node_rows, features = nodes.shape
    edge_rows = edges.shape[0]
    layers = edge_w1.shape[0]
    hot_width = -(-2 * plan.others // LANES) * LANES
    own_width = -(-2 * plan.near // LANES) * LANES
    wide = (edge_rows, features)
    lines, columns = range(1, plan.lines), range(1, plan.columns)
    own_shape = near_by((plan.near_total + plan.line_rows, features))
    kept_shape = near_by((plan.near + plan.column_rows, features))
    far_shape = near_by((plan.column_rows, features))
    line_shapes = [near_by((plan.line_message(a), features)) for a in lines]
    column_shapes = [near_by((plan.column_message(e), features)) for e in columns]
    weight_shapes = [near_by((2 * features, features)), near_by((features, features))]

    def local(arrays):
        return [(LOCAL, array) for array in arrays]

    def away(arrays):
        return [(AWAY, stay(array)) for array in arrays]

    small = cost(4 * plan.slots * node_rows * features, 4 * plan.slots * features)
    tables = [near_table, far_table]
    own, *lines_out = call(
        functools.partial(place_kernel, plan),
        "place",
        8,
        away([nodes, *tables]),
        local([own_shape, *line_shapes]),
        small,
        [
            pltpu.VMEM(far_table.shape, jnp.int32),
            pltpu.VMEM(near_table.shape, jnp.int32),
            pltpu.VMEM(nodes.shape, NARROW),
            pltpu.SemaphoreType.DMA((3,)),
        ],
    )
    index_shape = (edge_rows // LANES, LANES)
    hot_rows, own_hot, flip, edge_state, node_first, node_second, *selections = call(
        functools.partial(hots_kernel, plan),
        "hots",
        8,
        away([edge_sender.reshape(index_shape), edge_receiver.reshape(index_shape), edges])
        + away([node_w1, node_w2, *tables]),
        local([near_by((edge_rows, hot_width)), near_by((edge_rows, own_width))])
        + local([near_by((plan.slots, edge_rows)), near_by(wide)])
        + local([near_by(node_w1.shape), near_by(node_w2.shape)])
        + local([near_by((node_rows, plan.slots)), near_by((plan.slots, node_rows))]),
        cost(2 * edge_rows * features * features, 8 * edge_rows * features),
        [
            pltpu.VMEM(near_table.shape, jnp.int32),
            pltpu.VMEM(far_table.shape, jnp.int32),
            pltpu.VMEM(index_shape, jnp.int32),
            pltpu.VMEM(index_shape, jnp.int32),
            pltpu.SemaphoreType.DMA((7,)),
        ],
    )
    states = nodes
    for layer in range(layers):
        last = layer == layers - 1
        lines_in = [along_node(block, a) for a, block in zip(lines, lines_out)]
        far_first, *columns_out = call(
            functools.partial(turn_out_kernel, plan),
            "turn_out",
            8,
            local([own, flip, *lines_in]),
            local([far_shape, *column_shapes]),
            small,
        )
        start, *weights = call(
            functools.partial(start_kernel, plan, layer),
            "start",
            8,
            local([edge_state, own_hot, own])
            + away([edge_w1, edge_w2, edge_b1])
            + local([far_first if layer == 0 else own]),
            local([near_by(wide), *weight_shapes]),
            cost(2 * edge_rows * features * features, 4 * edge_rows * features),
            [
                pltpu.VMEM((features, features), NARROW),
                pltpu.VMEM(edge_b1.shape, jnp.float32),
                pltpu.VMEM((own_width, features), NARROW),
                pltpu.SemaphoreType.DMA((4,)),
            ],
        )
        columns_in = [along_feat(block, e) for e, block in zip(columns, columns_out)]
        scratch = [
            pltpu.VMEM(wide, NARROW),
            pltpu.VMEM((hot_width, features), NARROW),
        ]
        edge_state, kept, *columns_back = call(
            functools.partial(edge_kernel, plan, layer),
            "edge",
            16,
            local([hot_rows, flip, start, edge_state, *weights, edge_gain, edge_shift])
            + local([far_first, *columns_in]),
            local([near_by(wide), kept_shape, *column_shapes]),
            cost(
                2 * edge_rows * features * (hot_width + features + plan.slots),
                10 * edge_rows * features,
            ),
            scratch,
        )
        columns_in = [along_feat(block, -e) for e, block in zip(columns, columns_back)]
        near_sums, *lines_back = call(
            functools.partial(turn_back_kernel, plan),
            "turn_back",
            8,
            local([kept, *columns_in]),
            local([own_shape, *line_shapes]),
            small,
        )
        lines_in = [along_node(block, -a) for a, block in zip(lines, lines_back)]
        out_shape = [jax.ShapeDtypeStruct(nodes.shape, NARROW)] if last else [near_by(nodes.shape)]
        outs = call(
            functools.partial(node_kernel, plan, layer, last),
            "node",
            8,
            local([states, *selections, near_sums, *lines_in])
            + local([node_first, node_b1, node_second, node_gain, node_shift]),
            local(out_shape + ([] if last else [own_shape, *line_shapes])),
            small,
        )
        states = outs[0]
        if not last:
            own, *lines_out = outs[1:]
    return (states, edge_state)


def solution(mesh):
    split = ("ens", "node", "feat")
    return jax.shard_map(
        on_device,
        mesh=mesh,
        in_specs=(
            P(split, None),
            P(split, None),
            P(split, None, None),
            P(split, None, None),
            P(split),
            P(split),
        )
        + (P(),) * 10,
        out_specs=(P(split, None), P(split, None)),
        check_vma=False,
    )
```
